512 devices in a mesh: rows: 64 (over x, z), cols: 8 (over y, core).
Axes of the slice: x: 4, y: 4, z: 16, core: 2. Of those that a mesh axis runs over, the one named last changes fastest.
Arguments:
- sketch: bfloat16 [131072, 256], P(('rows', 'cols')), may hold values from -6 to 6
- blocks: bfloat16 [4096, 256, 256], P(('rows', 'cols')), may hold values from -0.375 to 0.375
- block_rows: int32 [4096], P(('rows', 'cols')), may hold values from 0 to 3, as said below
- block_cols: int32 [4096], P(('rows', 'cols')), may hold values from 0 to 63
- counts: int32 [512], P(('rows', 'cols')), may hold values from 1 to 8, as said below
Outputs:
- basis: float32 [65536, 256], P(('rows', 'cols'))
- factor: float32 [256, 256], replicated
The draws below stay inside these ranges and needn't reach their ends.
Inputs may be any that keep to these rules, and one draw needn't show every extreme that they name: Within one device's 8 slots the pairs (block_rows, block_cols) are distinct. `counts`: some device has exactly 8 live slots.
All inputs are finite; a program needn't handle non-finite values.
Results may differ from the reference program's by a relative error of at most 0.0003.
Values may be sent and summed in bfloat16 or wider, within the bound.
A program may use at most 64 MiB of HBM per device.

```python
import jax
import jax.numpy as jnp
from jax import lax

V = 131072
BS = 256
K = 256
RB = 4
BLK = 8
M = 65536
PB = 64
N_ROWS = 64
N_COLS = 8


def positions(key):
    devices = N_ROWS * N_COLS
    keys = jax.random.split(jax.random.fold_in(key, 11), devices)
    picked = jax.vmap(lambda single: jax.random.permutation(single, RB * PB)[:BLK])(keys)
    return picked.reshape(devices * BLK).astype(jnp.int32)


def draw_block_rows(key, part):
    return (positions(key) // PB).astype(jnp.int32)


def draw_block_cols(key, part):
    return (positions(key) % PB).astype(jnp.int32)


def draw_counts(key, part):
    devices = N_ROWS * N_COLS
    first = jax.random.randint(jax.random.fold_in(key, 21), (devices,), 0, BLK)
    second = jax.random.randint(jax.random.fold_in(key, 22), (devices,), 0, BLK)
    busiest = jax.random.randint(jax.random.fold_in(key, 23), (), 0, devices)
    loads = 1 + jnp.minimum(first, second)
    return jnp.where(jnp.arange(devices, dtype=jnp.int32) == busiest, BLK, loads).astype(jnp.int32)


def levels(rng, shape, cuts, smallest, largest):
    factor_of, own = 1.0, jax.random.fold_in(rng, 6)
    for dim, shards_of in cuts:
        draws = jnp.exp(jax.random.uniform(jax.random.fold_in(own, dim), (shards_of,), jnp.float32, smallest / len(cuts), largest / len(cuts)))
        factor_of = factor_of * jnp.repeat(draws, shape[dim] // shards_of).reshape([-1 if axis == dim else 1 for axis in range(len(shape))])
    return factor_of


def bell_draw(stream_key, dims, deviation, reach, cuts=(), kind=jnp.bfloat16):
    drawn = deviation * jax.random.normal(stream_key, dims, jnp.float32)
    if cuts:
        drawn = drawn * levels(stream_key, dims, cuts, -0.22, 0.18)
    return jnp.clip(drawn, -reach, reach).astype(kind)


def setup_inputs(seed: int = 0) -> dict:
    seeds = jax.random.split(jax.random.key(seed), 6)
    return {
        "sketch": bell_draw(seeds[0], (V, K), 1.0, 6.0, ((0, 512),)),
        "blocks": bell_draw(seeds[1], (N_ROWS * N_COLS * BLK, BS, BS), BS ** -0.5, 0.375, ((0, 512),)),
        "block_rows": draw_block_rows(jax.random.fold_in(seeds[5], 71), 0),
        "block_cols": draw_block_cols(jax.random.fold_in(seeds[5], 71), 0),
        "counts": draw_counts(jax.random.fold_in(seeds[5], 71), 0),
    }


def reference(sketch, blocks, block_rows, block_cols, counts):
    group_rows = V // (N_ROWS * N_COLS)
    highest = lax.Precision.HIGHEST

    def slab_rows(row_index):

        def add_panel(column, total):
            device = row_index * N_COLS + column
            tiles = lax.dynamic_slice_in_dim(blocks, device * BLK, BLK, 0).astype(jnp.float32)
            row_ids = lax.dynamic_slice_in_dim(block_rows, device * BLK, BLK, 0)
            col_ids = lax.dynamic_slice_in_dim(block_cols, device * BLK, BLK, 0)
            live_count = lax.dynamic_index_in_dim(counts, device, 0, keepdims=False)
            offsets = (col_ids * BS // group_rows * N_COLS + column) * group_rows + col_ids * BS % group_rows
            chosen = jax.vmap(lambda offset: lax.dynamic_slice_in_dim(sketch, offset.astype(jnp.int32), BS, 0))(offsets)
            products = jnp.einsum('bij,bjk->bik', tiles, chosen.astype(jnp.float32), precision=highest)
            selector = ((row_ids[:, None] == jnp.arange(RB, dtype=jnp.int32)[None, :]) & (jnp.arange(BLK, dtype=jnp.int32) < live_count)[:, None]).astype(jnp.float32)
            return total + jnp.einsum('br,bik->rik', selector, products, precision=highest)
        return lax.fori_loop(0, N_COLS, add_panel, jnp.zeros((RB, BS, K), jnp.float32))
    sketched = lax.map(slab_rows, jnp.arange(N_ROWS, dtype=jnp.int32)).reshape(M, K)
    gram_matrix = jnp.dot(sketched.T, sketched, precision=highest)
    lower_factor = jnp.linalg.cholesky(gram_matrix)
    root_rows = jnp.sqrt(jnp.float32(M))
    solved = lax.linalg.triangular_solve(lower_factor, sketched, left_side=False, lower=True, transpose_a=True)
    return (solved * root_rows, lower_factor.T / root_rows)
```

```python
import functools

import jax
import jax.numpy as jnp
from jax import lax
from jax.experimental import pallas as pl
from jax.experimental.pallas import tpu as pltpu
from jax.sharding import PartitionSpec as P

MESH = pl.DeviceIdType.MESH
HIGHEST = lax.Precision.HIGHEST
RB = 4
NX, NZ, NY, NC = 4, 16, 4, 2
WIDTH = 256
SPLIT = 96
GROUP = 32
SHARE = 128


def copy_to(src, dst, send_sem, recv_sem, row, col):
    return pltpu.make_async_remote_copy(
        src_ref=src, dst_ref=dst, send_sem=send_sem, recv_sem=recv_sem,
        device_id=(row, col), device_id_type=MESH,
    )


def greet(peers):
    barrier = pltpu.get_barrier_semaphore()
    for row, col in peers:
        pl.semaphore_signal(barrier, inc=1, device_id=(row, col), device_id_type=MESH)
    pl.semaphore_wait(barrier, len(peers))


def sketch_kernel(
    rows_ref, cols_ref, counts_ref, sketch_ref, blocks_ref, own_ref, gram_ref,
    panel, partial, received, half, received2,
    local_sem, xa_send, xa_recv, za_send, za_recv, zb_send, zb_recv,
    xb_send, xb_recv, op_send, op_recv, c_send, c_recv, y_send, y_recv,
):
    r = lax.axis_index("rows")
    c = lax.axis_index("cols")
    x, z = r // NZ, lax.rem(r, NZ)
    y, core = c // NC, lax.rem(c, NC)

    def at_x(k):
        return lax.rem(x + k, NX) * NZ + z

    def at_z(k):
        return x * NZ + lax.rem(z + k, NZ)

    greet(
        [(at_x(k), c) for k in (1, 2, 3)]
        + [(at_z(1), c), (at_z(NZ - 1), c), (r, y * NC + 1 - core)]
        + [(r, lax.rem(y + k, NY) * NC + core) for k in (1, 2, 3)]
    )

    local = pltpu.make_async_copy(sketch_ref, panel.at[x, z], local_sem)
    local.start()
    local.wait()

    first = pl.ds(0, SPLIT)
    second = pl.ds(SPLIT, WIDTH - SPLIT)

    def shifted(k):
        return lax.rem(z + k + NZ, NZ)

    def xa(k):
        piece = panel.at[x, z, first]
        return copy_to(piece, piece, xa_send.at[k - 1], xa_recv.at[k - 1], at_x(k), c)

    def za(side, hop):
        step = 1 - 2 * side
        piece = panel.at[:, shifted(-step * (hop - 1)), first]
        to = at_z(1 if side == 0 else NZ - 1)
        return copy_to(piece, piece, za_send.at[side, hop - 1], za_recv.at[side, hop - 1], to, c)

    def za_arrived(side, hop):
        step = 1 - 2 * side
        piece = panel.at[:, shifted(-step * hop), first]
        to = at_z(1 if side == 0 else NZ - 1)
        copy_to(piece, piece, za_send.at[side, hop - 1], za_recv.at[side, hop - 1], to, c).wait_recv()

    def zb(side, hop):
        step = 1 - 2 * side
        piece = panel.at[x, shifted(-step * (hop - 1)), second]
        to = at_z(1 if side == 0 else NZ - 1)
        return copy_to(piece, piece, zb_send.at[side, hop - 1], zb_recv.at[side, hop - 1], to, c)

    def zb_arrived(side, hop):
        step = 1 - 2 * side
        piece = panel.at[x, shifted(-step * hop), second]
        to = at_z(1 if side == 0 else NZ - 1)
        copy_to(piece, piece, zb_send.at[side, hop - 1], zb_recv.at[side, hop - 1], to, c).wait_recv()

    def piece_of(family, slot, column):
        at = shifted(-slot - 1) if family == 0 else shifted(slot)
        return panel.at[column, at, second]

    def xb(family, slot, way):
        piece = piece_of(family, slot, x)
        to = at_x(1 if way == 0 else NX - 1)
        return copy_to(piece, piece, xb_send.at[family, way, slot], xb_recv.at[family, way, slot], to, c)

    def xb_arrived(family, slot, way):
        column = lax.rem(x + (NX - 1 if way == 0 else 1), NX)
        piece = piece_of(family, slot, column)
        to = at_x(1 if way == 0 else NX - 1)
        copy_to(piece, piece, xb_send.at[family, way, slot], xb_recv.at[family, way, slot], to, c).wait_recv()

    def op(family, slot):
        column = lax.rem(x + (NX - 1 if family == 0 else 1), NX)
        piece = piece_of(family, slot, column)
        to = at_x(1 if family == 0 else NX - 1)
        return copy_to(piece, piece, op_send.at[family, slot], op_recv.at[family, slot], to, c)

    def op_arrived(family, slot):
        piece = piece_of(family, slot, lax.rem(x + 2, NX))
        to = at_x(1 if family == 0 else NX - 1)
        copy_to(piece, piece, op_send.at[family, slot], op_recv.at[family, slot], to, c).wait_recv()

    for k in (1, 2, 3):
        xa(k).start()
    for side in (0, 1):
        zb(side, 1).start()
    for way in (0, 1):
        xb(1, 0, way).start()
    for k in (1, 2, 3):
        piece = panel.at[lax.rem(x + NX - k, NX), z, first]
        copy_to(piece, piece, xa_send.at[k - 1], xa_recv.at[k - 1], at_x(k), c).wait_recv()
    for side in (0, 1):
        za(side, 1).start()

    def hop_body(hop, carry):
        zb_arrived(0, hop)
        zb(0, hop + 1).start()
        for way in (0, 1):
            xb(0, hop - 1, way).start()
        zb_arrived(1, hop)

        @pl.when(hop < 7)
        def _():
            zb(1, hop + 1).start()

        for way in (0, 1):
            xb(1, hop, way).start()
        za_arrived(1, hop)
        za(1, hop + 1).start()
        za_arrived(0, hop)

        @pl.when(hop < 7)
        def _():
            za(0, hop + 1).start()

        xb_arrived(1, hop - 1, 1)
        op(1, hop - 1).start()

        @pl.when(hop > 1)
        def _():
            xb_arrived(0, hop - 2, 0)
            op(0, hop - 2).start()

        return carry

    lax.fori_loop(1, 8, hop_body, 0)
    zb_arrived(0, 8)
    for way in (0, 1):
        xb(0, 7, way).start()
    xb_arrived(1, 7, 1)
    op(1, 7).start()
    xb_arrived(0, 6, 0)
    op(0, 6).start()
    xb_arrived(0, 7, 0)
    op(0, 7).start()
    za_arrived(1, 8)

    def drain(slot, carry):
        xb_arrived(0, slot, 1)
        xb_arrived(1, slot, 0)
        for family in (0, 1):
            op_arrived(family, slot)
            op(family, slot).wait_send()
            for way in (0, 1):
                xb(family, slot, way).wait_send()
        zb(0, slot + 1).wait_send()
        za(1, slot + 1).wait_send()

        @pl.when(slot < 7)
        def _():
            zb(1, slot + 1).wait_send()
            za(0, slot + 1).wait_send()

        return carry

    lax.fori_loop(0, 8, drain, 0)
    for k in (1, 2, 3):
        xa(k).wait_send()

    partial[...] = jnp.zeros_like(partial)
    live = counts_ref[0]

    def slot_body(s, carry):
        q = cols_ref[s]
        product = jnp.dot(
            blocks_ref[s], panel[q // NZ, lax.rem(q, NZ)], preferred_element_type=jnp.float32
        )
        for b in range(RB):
            weight = jnp.where(jnp.logical_and(rows_ref[s] == b, s < live), 1.0, 0.0)
            for part in range(NC):
                partial[b, part] += weight * product[part * SHARE:(part + 1) * SHARE]
        return carry

    lax.fori_loop(0, 8, slot_body, 0)

    pair = copy_to(partial.at[:, 1 - core], received, c_send, c_recv, r, y * NC + 1 - core)
    pair.start()
    pair.wait()
    half[...] = partial[:, core] + received[...]
    sends = []
    for k in (1, 2, 3):
        other = lax.rem(y + k, NY)
        send = copy_to(
            half.at[other], received2.at[k - 1], y_send.at[k - 1], y_recv.at[k - 1], r, other * NC + core
        )
        send.start()
        sends.append(send)
    for send in sends:
        send.wait()
    own = half[y] + received2[0] + received2[1] + received2[2]
    own_ref[...] = own
    gram_ref[...] = lax.dot_general(
        own, own, (((0,), (0,)), ((), ())), precision=HIGHEST, preferred_element_type=jnp.float32
    )


def sum_kernel(gram_ref, out_ref, slots, lines, a_send, a_recv, z_send, z_recv, b_send, b_recv):
    r = lax.axis_index("rows")
    c = lax.axis_index("cols")
    x, z = r // NZ, lax.rem(r, NZ)
    cols = NY * NC
    me = x * cols + c

    def member(k):
        other = lax.rem(me + k, GROUP)
        return other, (other // cols) * NZ + z, lax.rem(other, cols)

    def along(k):
        return x * NZ + lax.rem(z + k, NZ)

    barrier = pltpu.get_barrier_semaphore()

    def hello_group(k, carry):
        _, row, col = member(k)
        pl.semaphore_signal(barrier, inc=1, device_id=(row, col), device_id_type=MESH)
        return carry

    def hello_line(k, carry):
        pl.semaphore_signal(barrier, inc=1, device_id=(along(k), c), device_id_type=MESH)
        return carry

    lax.fori_loop(1, GROUP, hello_group, 0)
    lax.fori_loop(1, NZ, hello_line, 0)
    pl.semaphore_wait(barrier, GROUP - 1 + NZ - 1)

    def scatter(k):
        other, row, col = member(k)
        return copy_to(gram_ref.at[other], slots.at[k - 1], a_send.at[k - 1], a_recv.at[k - 1], row, col)

    def line(k):
        return copy_to(lines.at[z], lines.at[z], z_send.at[k - 1], z_recv.at[k - 1], along(k), c)

    def line_arrived(k):
        source = lax.rem(z + NZ - k, NZ)
        copy_to(
            lines.at[source], lines.at[source], z_send.at[k - 1], z_recv.at[k - 1], along(k), c
        ).wait_recv()

    def spread(k):
        _, row, col = member(k)
        return copy_to(out_ref.at[me], out_ref.at[me], b_send.at[k - 1], b_recv.at[k - 1], row, col)

    def spread_arrived(k):
        _, row, col = member(k)
        source = lax.rem(me + GROUP - k, GROUP)
        copy_to(
            out_ref.at[source], out_ref.at[source], b_send.at[k - 1], b_recv.at[k - 1], row, col
        ).wait_recv()

    def loop(start, stop, act):
        def body(k, carry):
            act(k)
            return carry
        lax.fori_loop(start, stop, body, 0)

    loop(1, GROUP, lambda k: scatter(k).start())
    loop(1, GROUP, lambda k: scatter(k).wait())
    lines[z] = gram_ref[me] + jnp.sum(slots[...], axis=0)
    loop(1, NZ, lambda k: line(k).start())
    loop(1, NZ, line_arrived)
    out_ref[me] = jnp.sum(lines[...], axis=0)
    loop(1, GROUP, lambda k: spread(k).start())
    loop(1, GROUP, spread_arrived)
    loop(1, NZ, lambda k: line(k).wait_send())
    loop(1, GROUP, lambda k: spread(k).wait_send())


def local(sketch, blocks, block_rows, block_cols, counts):
    f32 = jnp.float32
    dma = pltpu.SemaphoreType.DMA
    vmem = pl.BlockSpec(memory_space=pltpu.VMEM)
    smem = pl.BlockSpec(memory_space=pltpu.SMEM)
    own, gram = pl.pallas_call(
        sketch_kernel,
        out_shape=(
            jax.ShapeDtypeStruct((SHARE, WIDTH), f32),
            jax.ShapeDtypeStruct((WIDTH, WIDTH), f32),
        ),
        in_specs=[smem, smem, smem, vmem, vmem],
        out_specs=(vmem, vmem),
        scratch_shapes=[
            pltpu.VMEM((NX, NZ, WIDTH, WIDTH), jnp.bfloat16),
            pltpu.VMEM((RB, NC, SHARE, WIDTH), f32),
            pltpu.VMEM((RB, SHARE, WIDTH), f32),
            pltpu.VMEM((RB, SHARE, WIDTH), f32),
            pltpu.VMEM((NY - 1, SHARE, WIDTH), f32),
            dma,
            dma((3,)), dma((3,)),
            dma((2, 8)), dma((2, 8)),
            dma((2, 8)), dma((2, 8)),
            dma((2, 2, 8)), dma((2, 2, 8)),
            dma((2, 8)), dma((2, 8)),
            dma, dma,
            dma((3,)), dma((3,)),
        ],
        compiler_params=pltpu.CompilerParams(collective_id=0, has_side_effects=True),
        name="sketch",
    )(block_rows, block_cols, counts, sketch, blocks)
    gram = pl.pallas_call(
        sum_kernel,
        out_shape=jax.ShapeDtypeStruct((GROUP, 8, WIDTH), f32),
        in_specs=[vmem],
        out_specs=vmem,
        scratch_shapes=[
            pltpu.VMEM((GROUP - 1, 8, WIDTH), f32),
            pltpu.VMEM((NZ, 8, WIDTH), f32),
            dma((GROUP - 1,)), dma((GROUP - 1,)),
            dma((NZ - 1,)), dma((NZ - 1,)),
            dma((GROUP - 1,)), dma((GROUP - 1,)),
        ],
        compiler_params=pltpu.CompilerParams(collective_id=1, has_side_effects=True),
        name="gram_sum",
    )(gram.reshape(GROUP, 8, WIDTH)).reshape(WIDTH, WIDTH)
    lower_factor = jnp.linalg.cholesky(gram)
    root_rows = jnp.sqrt(f32(RB * WIDTH * lax.axis_size("rows")))
    solved = lax.linalg.triangular_solve(
        lower_factor, own, left_side=False, lower=True, transpose_a=True
    )
    return (solved * root_rows, lower_factor.T / root_rows)


def solution(mesh):
    in_specs = (
        P(("rows", "cols"), None),
        P(("rows", "cols"), None, None),
        P(("rows", "cols")),
        P(("rows", "cols")),
        P(("rows", "cols")),
    )
    out_specs = (P(("rows", "cols"), None), P())
    return jax.shard_map(local, mesh=mesh, in_specs=in_specs, out_specs=out_specs, check_vma=False)
```

```python
import functools

import jax
import jax.numpy as jnp
from jax import lax
from jax.experimental import pallas as pl
from jax.experimental.pallas import tpu as pltpu
from jax.sharding import PartitionSpec as P

MESH = pl.DeviceIdType.MESH
HIGHEST = lax.Precision.HIGHEST
RB = 4
NX, NZ, NY, NC = 4, 16, 4, 2
WIDTH = 256
SPLIT = 96
GROUP = 32
SHARE = 128
HALF = 128


def copy_to(src, dst, send_sem, recv_sem, row, col):
    return pltpu.make_async_remote_copy(
        src_ref=src, dst_ref=dst, send_sem=send_sem, recv_sem=recv_sem,
        device_id=(row, col), device_id_type=MESH,
    )


def greet(peers):
    barrier = pltpu.get_barrier_semaphore()
    for row, col in peers:
        pl.semaphore_signal(barrier, inc=1, device_id=(row, col), device_id_type=MESH)
    pl.semaphore_wait(barrier, len(peers))


def sketch_kernel(
    rows_ref, cols_ref, counts_ref, sketch_ref, blocks_ref, own_ref, gram_ref,
    panel, partial, received, half, received2,
    local_sem, xa_send, xa_recv, za_send, za_recv, zb_send, zb_recv,
    xb_send, xb_recv, op_send, op_recv, c_send, c_recv, y_send, y_recv,
):
    r = lax.axis_index("rows")
    c = lax.axis_index("cols")
    x, z = r // NZ, lax.rem(r, NZ)
    y, core = c // NC, lax.rem(c, NC)

    def at_x(k):
        return lax.rem(x + k, NX) * NZ + z

    def at_z(k):
        return x * NZ + lax.rem(z + k, NZ)

    greet(
        [(at_x(k), c) for k in (1, 2, 3)]
        + [(at_z(1), c), (at_z(NZ - 1), c), (r, y * NC + 1 - core)]
        + [(r, lax.rem(y + k, NY) * NC + core) for k in (1, 2, 3)]
    )

    local = pltpu.make_async_copy(sketch_ref, panel.at[x, z], local_sem)
    local.start()
    local.wait()

    first = pl.ds(0, SPLIT)
    second = pl.ds(SPLIT, WIDTH - SPLIT)

    def shifted(k):
        return lax.rem(z + k + NZ, NZ)

    def xa(k):
        piece = panel.at[x, z, first]
        return copy_to(piece, piece, xa_send.at[k - 1], xa_recv.at[k - 1], at_x(k), c)

    def za(side, hop):
        step = 1 - 2 * side
        piece = panel.at[:, shifted(-step * (hop - 1)), first]
        to = at_z(1 if side == 0 else NZ - 1)
        return copy_to(piece, piece, za_send.at[side, hop - 1], za_recv.at[side, hop - 1], to, c)

    def za_arrived(side, hop):
        step = 1 - 2 * side
        piece = panel.at[:, shifted(-step * hop), first]
        to = at_z(1 if side == 0 else NZ - 1)
        copy_to(piece, piece, za_send.at[side, hop - 1], za_recv.at[side, hop - 1], to, c).wait_recv()

    def zb(side, hop):
        step = 1 - 2 * side
        piece = panel.at[x, shifted(-step * (hop - 1)), second]
        to = at_z(1 if side == 0 else NZ - 1)
        return copy_to(piece, piece, zb_send.at[side, hop - 1], zb_recv.at[side, hop - 1], to, c)

    def zb_arrived(side, hop):
        step = 1 - 2 * side
        piece = panel.at[x, shifted(-step * hop), second]
        to = at_z(1 if side == 0 else NZ - 1)
        copy_to(piece, piece, zb_send.at[side, hop - 1], zb_recv.at[side, hop - 1], to, c).wait_recv()

    def piece_of(family, slot, column):
        at = shifted(-slot - 1) if family == 0 else shifted(slot)
        return panel.at[column, at, second]

    def xb(family, slot, way):
        piece = piece_of(family, slot, x)
        to = at_x(1 if way == 0 else NX - 1)
        return copy_to(piece, piece, xb_send.at[family, way, slot], xb_recv.at[family, way, slot], to, c)

    def xb_arrived(family, slot, way):
        column = lax.rem(x + (NX - 1 if way == 0 else 1), NX)
        piece = piece_of(family, slot, column)
        to = at_x(1 if way == 0 else NX - 1)
        copy_to(piece, piece, xb_send.at[family, way, slot], xb_recv.at[family, way, slot], to, c).wait_recv()

    def op(family, slot):
        column = lax.rem(x + (NX - 1 if family == 0 else 1), NX)
        piece = piece_of(family, slot, column)
        to = at_x(1 if family == 0 else NX - 1)
        return copy_to(piece, piece, op_send.at[family, slot], op_recv.at[family, slot], to, c)

    def op_arrived(family, slot):
        piece = piece_of(family, slot, lax.rem(x + 2, NX))
        to = at_x(1 if family == 0 else NX - 1)
        copy_to(piece, piece, op_send.at[family, slot], op_recv.at[family, slot], to, c).wait_recv()

    for k in (1, 2, 3):
        xa(k).start()
    for side in (0, 1):
        zb(side, 1).start()
    for way in (0, 1):
        xb(1, 0, way).start()
    for k in (1, 2, 3):
        piece = panel.at[lax.rem(x + NX - k, NX), z, first]
        copy_to(piece, piece, xa_send.at[k - 1], xa_recv.at[k - 1], at_x(k), c).wait_recv()
    for side in (0, 1):
        za(side, 1).start()

    def hop_body(hop, carry):
        zb_arrived(0, hop)
        zb(0, hop + 1).start()
        for way in (0, 1):
            xb(0, hop - 1, way).start()
        zb_arrived(1, hop)

        @pl.when(hop < 7)
        def _():
            zb(1, hop + 1).start()

        for way in (0, 1):
            xb(1, hop, way).start()
        za_arrived(1, hop)
        za(1, hop + 1).start()
        za_arrived(0, hop)

        @pl.when(hop < 7)
        def _():
            za(0, hop + 1).start()

        xb_arrived(1, hop - 1, 1)
        op(1, hop - 1).start()

        @pl.when(hop > 1)
        def _():
            xb_arrived(0, hop - 2, 0)
            op(0, hop - 2).start()

        return carry

    lax.fori_loop(1, 8, hop_body, 0)
    zb_arrived(0, 8)
    for way in (0, 1):
        xb(0, 7, way).start()
    xb_arrived(1, 7, 1)
    op(1, 7).start()
    xb_arrived(0, 6, 0)
    op(0, 6).start()
    xb_arrived(0, 7, 0)
    op(0, 7).start()
    za_arrived(1, 8)

    def drain(slot, carry):
        xb_arrived(0, slot, 1)
        xb_arrived(1, slot, 0)
        for family in (0, 1):
            op_arrived(family, slot)
            op(family, slot).wait_send()
            for way in (0, 1):
                xb(family, slot, way).wait_send()
        zb(0, slot + 1).wait_send()
        za(1, slot + 1).wait_send()

        @pl.when(slot < 7)
        def _():
            zb(1, slot + 1).wait_send()
            za(0, slot + 1).wait_send()

        return carry

    lax.fori_loop(0, 8, drain, 0)
    for k in (1, 2, 3):
        xa(k).wait_send()

    partial[...] = jnp.zeros_like(partial)
    live = counts_ref[0]

    def slot_body(s, carry):
        q = cols_ref[s]
        product = jnp.dot(
            blocks_ref[s], panel[q // NZ, lax.rem(q, NZ)], preferred_element_type=jnp.float32
        )
        for b in range(RB):
            weight = jnp.where(jnp.logical_and(rows_ref[s] == b, s < live), 1.0, 0.0)
            for part in range(NC):
                partial[b, part] += weight * product[part * SHARE:(part + 1) * SHARE]
        return carry

    lax.fori_loop(0, 8, slot_body, 0)

    pair = copy_to(partial.at[:, 1 - core], received, c_send, c_recv, r, y * NC + 1 - core)
    pair.start()
    pair.wait()
    half[...] = partial[:, core] + received[...]
    sends = []
    for k in (1, 2, 3):
        other = lax.rem(y + k, NY)
        send = copy_to(
            half.at[other], received2.at[k - 1], y_send.at[k - 1], y_recv.at[k - 1], r, other * NC + core
        )
        send.start()
        sends.append(send)
    for send in sends:
        send.wait()
    own = half[y] + received2[0] + received2[1] + received2[2]
    own_ref[...] = own
    gram_ref[...] = lax.dot_general(
        own, own, (((0,), (0,)), ((), ())), precision=HIGHEST, preferred_element_type=jnp.float32
    )


def sum_kernel(gram_ref, out_ref, slots, lines, a_send, a_recv, z_send, z_recv, b_send, b_recv):
    r = lax.axis_index("rows")
    c = lax.axis_index("cols")
    x, z = r // NZ, lax.rem(r, NZ)
    cols = NY * NC
    me = x * cols + c

    def member(k):
        other = lax.rem(me + k, GROUP)
        return other, (other // cols) * NZ + z, lax.rem(other, cols)

    def along(k):
        return x * NZ + lax.rem(z + k, NZ)

    barrier = pltpu.get_barrier_semaphore()

    def hello_group(k, carry):
        _, row, col = member(k)
        pl.semaphore_signal(barrier, inc=1, device_id=(row, col), device_id_type=MESH)
        return carry

    def hello_line(k, carry):
        pl.semaphore_signal(barrier, inc=1, device_id=(along(k), c), device_id_type=MESH)
        return carry

    lax.fori_loop(1, GROUP, hello_group, 0)
    lax.fori_loop(1, NZ, hello_line, 0)
    pl.semaphore_wait(barrier, GROUP - 1 + NZ - 1)

    def scatter(k):
        other, row, col = member(k)
        return copy_to(gram_ref.at[other], slots.at[k - 1], a_send.at[k - 1], a_recv.at[k - 1], row, col)

    def line(k):
        return copy_to(lines.at[z], lines.at[z], z_send.at[k - 1], z_recv.at[k - 1], along(k), c)

    def line_arrived(k):
        source = lax.rem(z + NZ - k, NZ)
        copy_to(
            lines.at[source], lines.at[source], z_send.at[k - 1], z_recv.at[k - 1], along(k), c
        ).wait_recv()

    def spread(k):
        _, row, col = member(k)
        return copy_to(out_ref.at[me], out_ref.at[me], b_send.at[k - 1], b_recv.at[k - 1], row, col)

    def spread_arrived(k):
        _, row, col = member(k)
        source = lax.rem(me + GROUP - k, GROUP)
        copy_to(
            out_ref.at[source], out_ref.at[source], b_send.at[k - 1], b_recv.at[k - 1], row, col
        ).wait_recv()

    def loop(start, stop, act):
        def body(k, carry):
            act(k)
            return carry
        lax.fori_loop(start, stop, body, 0)

    loop(1, GROUP, lambda k: scatter(k).start())
    loop(1, GROUP, lambda k: scatter(k).wait())
    lines[z] = gram_ref[me] + jnp.sum(slots[...], axis=0)
    loop(1, NZ, lambda k: line(k).start())
    loop(1, NZ, line_arrived)
    out_ref[me] = jnp.sum(lines[...], axis=0)
    loop(1, GROUP, lambda k: spread(k).start())
    loop(1, GROUP, spread_arrived)
    loop(1, NZ, lambda k: line(k).wait_send())
    loop(1, GROUP, lambda k: spread(k).wait_send())


def factor_kernel(step, root, gram_ref, own_ref, basis_ref, factor_ref, work, rows):
    f32 = jnp.float32
    lane = lax.broadcasted_iota(jnp.int32, (1, HALF), 1)
    below = lax.broadcasted_iota(jnp.int32, (HALF, HALF), 0) > lax.broadcasted_iota(
        jnp.int32, (HALF, HALF), 1
    )
    eye = (
        lax.broadcasted_iota(jnp.int32, (HALF, HALF), 0)
        == lax.broadcasted_iota(jnp.int32, (HALF, HALF), 1)
    ).astype(f32)

    def dot(a, b, dims):
        return lax.dot_general(a, b, (dims, ((), ())), precision=HIGHEST, preferred_element_type=f32)

    def pick(value, j):
        return jnp.sum(jnp.where(lane == j, value, 0.0), axis=1, keepdims=True)

    def eliminate(block):
        work[:, :HALF] = block
        work[:, HALF:] = eye

        def body(i, carry):
            j = i * step
            line = [work[pl.ds(j + t, 1), :] for t in range(step)]
            column = [pick(work[:, :HALF], j + t) for t in range(step)]
            entry = [[pick(line[t][:, :HALF], j + u) for u in range(step)] for t in range(step)]
            scaled = []
            for t in range(step):
                inverse = 1.0 / entry[t][t]
                for u in range(t + 1, step):
                    ratio = entry[t][u] * inverse
                    line[u] = line[u] - ratio * line[t]
                    column[u] = column[u] - ratio * column[t]
                    for v in range(u, step):
                        entry[u][v] = entry[u][v] - ratio * entry[t][v]
                scaled.append(line[t] * inverse)
            total = work[...]
            for t in range(step):
                total = total - column[t] * scaled[t]
            work[...] = total
            for t in range(step):
                rows[pl.ds(j + t, 1), :] = line[t] * (1.0 / jnp.sqrt(entry[t][t]))
            return carry

        lax.fori_loop(0, HALF // step, body, 0)
        return jnp.where(below, 0.0, rows[:, :HALF]), rows[:, HALF:]

    upper1, inverse1 = eliminate(gram_ref[:HALF, :HALF])
    cross = dot(inverse1, gram_ref[:HALF, HALF:], ((1,), (0,)))
    factor_ref[:HALF, :HALF] = upper1 * (1.0 / root)
    factor_ref[:HALF, HALF:] = cross * (1.0 / root)
    factor_ref[HALF:, :HALF] = jnp.zeros((HALF, HALF), f32)
    solved = dot(own_ref[:, :HALF], inverse1, ((1,), (1,)))
    basis_ref[:, :HALF] = solved * root
    rest = own_ref[:, HALF:] - dot(solved, cross, ((1,), (0,)))
    schur = gram_ref[HALF:, HALF:] - dot(cross, cross, ((0,), (0,)))
    upper2, inverse2 = eliminate(schur)
    factor_ref[HALF:, HALF:] = upper2 * (1.0 / root)
    basis_ref[:, HALF:] = dot(rest, inverse2, ((1,), (1,))) * root


def factorize(gram, own, step):
    root = float(RB * WIDTH * NX * NZ) ** 0.5
    f32 = jnp.float32
    vmem = pl.BlockSpec(memory_space=pltpu.VMEM)
    return pl.pallas_call(
        functools.partial(factor_kernel, step, root),
        out_shape=(
            jax.ShapeDtypeStruct((SHARE, WIDTH), f32),
            jax.ShapeDtypeStruct((WIDTH, WIDTH), f32),
        ),
        in_specs=[vmem, vmem],
        out_specs=(vmem, vmem),
        scratch_shapes=[pltpu.VMEM((HALF, WIDTH), f32), pltpu.VMEM((HALF, WIDTH), f32)],
        name="factorize",
    )(gram, own)


def local(sketch, blocks, block_rows, block_cols, counts):
    f32 = jnp.float32
    dma = pltpu.SemaphoreType.DMA
    vmem = pl.BlockSpec(memory_space=pltpu.VMEM)
    smem = pl.BlockSpec(memory_space=pltpu.SMEM)
    own, gram = pl.pallas_call(
        sketch_kernel,
        out_shape=(
            jax.ShapeDtypeStruct((SHARE, WIDTH), f32),
            jax.ShapeDtypeStruct((WIDTH, WIDTH), f32),
        ),
        in_specs=[smem, smem, smem, vmem, vmem],
        out_specs=(vmem, vmem),
        scratch_shapes=[
            pltpu.VMEM((NX, NZ, WIDTH, WIDTH), jnp.bfloat16),
            pltpu.VMEM((RB, NC, SHARE, WIDTH), f32),
            pltpu.VMEM((RB, SHARE, WIDTH), f32),
            pltpu.VMEM((RB, SHARE, WIDTH), f32),
            pltpu.VMEM((NY - 1, SHARE, WIDTH), f32),
            dma,
            dma((3,)), dma((3,)),
            dma((2, 8)), dma((2, 8)),
            dma((2, 8)), dma((2, 8)),
            dma((2, 2, 8)), dma((2, 2, 8)),
            dma((2, 8)), dma((2, 8)),
            dma, dma,
            dma((3,)), dma((3,)),
        ],
        compiler_params=pltpu.CompilerParams(collective_id=0, has_side_effects=True),
        name="sketch",
    )(block_rows, block_cols, counts, sketch, blocks)
    gram = pl.pallas_call(
        sum_kernel,
        out_shape=jax.ShapeDtypeStruct((GROUP, 8, WIDTH), f32),
        in_specs=[vmem],
        out_specs=vmem,
        scratch_shapes=[
            pltpu.VMEM((GROUP - 1, 8, WIDTH), f32),
            pltpu.VMEM((NZ, 8, WIDTH), f32),
            dma((GROUP - 1,)), dma((GROUP - 1,)),
            dma((NZ - 1,)), dma((NZ - 1,)),
            dma((GROUP - 1,)), dma((GROUP - 1,)),
        ],
        compiler_params=pltpu.CompilerParams(collective_id=1, has_side_effects=True),
        name="gram_sum",
    )(gram.reshape(GROUP, 8, WIDTH)).reshape(WIDTH, WIDTH)
    return factorize(gram, own, 4)


def solution(mesh):
    in_specs = (
        P(("rows", "cols"), None),
        P(("rows", "cols"), None, None),
        P(("rows", "cols")),
        P(("rows", "cols")),
        P(("rows", "cols")),
    )
    out_specs = (P(("rows", "cols"), None), P())
    return jax.shard_map(local, mesh=mesh, in_specs=in_specs, out_specs=out_specs, check_vma=False)
```

```python
import functools

import jax
import jax.numpy as jnp
from jax import lax
from jax.experimental import pallas as pl
from jax.experimental.pallas import tpu as pltpu
from jax.sharding import PartitionSpec as P

MESH = pl.DeviceIdType.MESH
HIGHEST = lax.Precision.HIGHEST
RB = 4
NX, NZ, NY, NC = 4, 16, 4, 2
WIDTH = 256
SPLIT = 80
GROUP, LINE = 32, 4
SHARE = 128
HALF = 128


def copy_to(src, dst, send_sem, recv_sem, row, col):
    return pltpu.make_async_remote_copy(
        src_ref=src, dst_ref=dst, send_sem=send_sem, recv_sem=recv_sem,
        device_id=(row, col), device_id_type=MESH,
    )


def sketch_kernel(
    rows_ref, cols_ref, counts_ref, sketch_ref, blocks_ref, own_ref, gram_ref,
    panel, products, partial, received, half, received2, gram, slots, lows, highs,
    local_sem, xa_send, xa_recv, za_send, za_recv, zb_send, zb_recv,
    xb_send, xb_recv, op_send, op_recv, c_send, c_recv, y_send, y_recv,
    g_send, g_recv, l_send, l_recv, h_send, h_recv, s_send, s_recv,
):
    r = lax.axis_index("rows")
    c = lax.axis_index("cols")
    x, z = r // NZ, lax.rem(r, NZ)
    y, core = c // NC, lax.rem(c, NC)

    def at_x(k):
        return lax.rem(x + k, NX) * NZ + z

    def at_z(k):
        return x * NZ + lax.rem(z + k, NZ)

    cols = NY * NC
    me = x * cols + c
    low, high = lax.rem(z, LINE), z // LINE

    def member(k):
        other = lax.rem(me + k, GROUP)
        return other, (other // cols) * NZ + z, lax.rem(other, cols)

    def at_low(k):
        return x * NZ + high * LINE + lax.rem(low + k, LINE)

    def at_high(k):
        return x * NZ + lax.rem(high + k, LINE) * LINE + low

    barrier = pltpu.get_barrier_semaphore()

    def hello(row, col):
        pl.semaphore_signal(barrier, inc=1, device_id=(row, col), device_id_type=MESH)

    def hello_group(k, carry):
        _, row, col = member(k)
        hello(row, col)
        return carry

    for row in (at_z(1), at_z(NZ - 1)):
        hello(row, c)
    for k in range(1, LINE):
        hello(at_low(k), c)
        hello(at_high(k), c)
    lax.fori_loop(1, GROUP, hello_group, 0)
    pl.semaphore_wait(barrier, 2 + 2 * (LINE - 1) + GROUP - 1)

    local = pltpu.make_async_copy(sketch_ref, panel.at[x, z], local_sem)
    local.start()
    local.wait()

    first = pl.ds(0, SPLIT)
    second = pl.ds(SPLIT, WIDTH - SPLIT)

    def shifted(k):
        return lax.rem(z + k + NZ, NZ)

    def xa(k):
        piece = panel.at[x, z, first]
        return copy_to(piece, piece, xa_send.at[k - 1], xa_recv.at[k - 1], at_x(k), c)

    def za(side, hop):
        step = 1 - 2 * side
        piece = panel.at[:, shifted(-step * (hop - 1)), first]
        to = at_z(1 if side == 0 else NZ - 1)
        return copy_to(piece, piece, za_send.at[side, hop - 1], za_recv.at[side, hop - 1], to, c)

    def za_arrived(side, hop):
        step = 1 - 2 * side
        piece = panel.at[:, shifted(-step * hop), first]
        to = at_z(1 if side == 0 else NZ - 1)
        copy_to(piece, piece, za_send.at[side, hop - 1], za_recv.at[side, hop - 1], to, c).wait_recv()

    def zb(side, hop):
        step = 1 - 2 * side
        piece = panel.at[x, shifted(-step * (hop - 1)), second]
        to = at_z(1 if side == 0 else NZ - 1)
        return copy_to(piece, piece, zb_send.at[side, hop - 1], zb_recv.at[side, hop - 1], to, c)

    def zb_arrived(side, hop):
        step = 1 - 2 * side
        piece = panel.at[x, shifted(-step * hop), second]
        to = at_z(1 if side == 0 else NZ - 1)
        copy_to(piece, piece, zb_send.at[side, hop - 1], zb_recv.at[side, hop - 1], to, c).wait_recv()

    def piece_of(family, slot, column):
        at = shifted(-slot - 1) if family == 0 else shifted(slot)
        return panel.at[column, at, second]

    def xb(family, slot, way):
        piece = piece_of(family, slot, x)
        to = at_x(1 if way == 0 else NX - 1)
        return copy_to(piece, piece, xb_send.at[family, way, slot], xb_recv.at[family, way, slot], to, c)

    def xb_arrived(family, slot, way):
        column = lax.rem(x + (NX - 1 if way == 0 else 1), NX)
        piece = piece_of(family, slot, column)
        to = at_x(1 if way == 0 else NX - 1)
        copy_to(piece, piece, xb_send.at[family, way, slot], xb_recv.at[family, way, slot], to, c).wait_recv()

    def op(family, slot):
        column = lax.rem(x + (NX - 1 if family == 0 else 1), NX)
        piece = piece_of(family, slot, column)
        to = at_x(1 if family == 0 else NX - 1)
        return copy_to(piece, piece, op_send.at[family, slot], op_recv.at[family, slot], to, c)

    def op_arrived(family, slot):
        piece = piece_of(family, slot, lax.rem(x + 2, NX))
        to = at_x(1 if family == 0 else NX - 1)
        copy_to(piece, piece, op_send.at[family, slot], op_recv.at[family, slot], to, c).wait_recv()

    for k in (1, 2, 3):
        xa(k).start()
    for side in (0, 1):
        zb(side, 1).start()
    for way in (0, 1):
        xb(1, 0, way).start()
    for k in (1, 2, 3):
        piece = panel.at[lax.rem(x + NX - k, NX), z, first]
        copy_to(piece, piece, xa_send.at[k - 1], xa_recv.at[k - 1], at_x(k), c).wait_recv()
    for side in (0, 1):
        za(side, 1).start()

    def hop_body(hop, carry):
        zb_arrived(0, hop)
        zb(0, hop + 1).start()
        for way in (0, 1):
            xb(0, hop - 1, way).start()
        zb_arrived(1, hop)

        @pl.when(hop < 7)
        def _():
            zb(1, hop + 1).start()

        for way in (0, 1):
            xb(1, hop, way).start()
        za_arrived(1, hop)
        za(1, hop + 1).start()
        za_arrived(0, hop)

        @pl.when(hop < 7)
        def _():
            za(0, hop + 1).start()

        xb_arrived(1, hop - 1, 1)
        op(1, hop - 1).start()

        @pl.when(hop > 1)
        def _():
            xb_arrived(0, hop - 2, 0)
            op(0, hop - 2).start()

        return carry

    lax.fori_loop(1, 8, hop_body, 0)
    zb_arrived(0, 8)
    for way in (0, 1):
        xb(0, 7, way).start()
    xb_arrived(1, 7, 1)
    op(1, 7).start()
    xb_arrived(0, 6, 0)
    op(0, 6).start()
    xb_arrived(0, 7, 0)
    op(0, 7).start()
    za_arrived(1, 8)

    def drain(slot, carry):
        xb_arrived(0, slot, 1)
        xb_arrived(1, slot, 0)
        for family in (0, 1):
            op_arrived(family, slot)
            op(family, slot).wait_send()
            for way in (0, 1):
                xb(family, slot, way).wait_send()
        zb(0, slot + 1).wait_send()
        za(1, slot + 1).wait_send()

        @pl.when(slot < 7)
        def _():
            zb(1, slot + 1).wait_send()
            za(0, slot + 1).wait_send()

        return carry

    lax.fori_loop(0, 8, drain, 0)
    for k in (1, 2, 3):
        xa(k).wait_send()

    live = counts_ref[0]

    def slot_body(s, carry):
        q = cols_ref[s]
        products[s] = jnp.dot(
            blocks_ref[s], panel[q // NZ, lax.rem(q, NZ)], preferred_element_type=jnp.float32
        )
        return carry

    lax.fori_loop(0, 8, slot_body, 0)

    def pair(b):
        return copy_to(
            partial.at[b, 1 - core], received.at[b], c_send.at[b], c_recv.at[b], r, y * NC + 1 - core
        )

    def to_y(k):
        other = lax.rem(y + k, NY)
        return copy_to(
            half.at[other], received2.at[k - 1], y_send.at[k - 1], y_recv.at[k - 1], r, other * NC + core
        )

    def finish(k):
        b = lax.rem(y + k, NY)
        pair(b).wait_recv()
        half[b] = partial[b, core] + received[b]
        if k:
            to_y(k).start()

    order = (2, 1, 3, 0)
    for place, k in enumerate(order):
        b = lax.rem(y + k, NY)
        for part in range(NC):
            total = jnp.zeros((SHARE, WIDTH), jnp.float32)
            for s in range(8):
                weight = jnp.where(jnp.logical_and(rows_ref[s] == b, s < live), 1.0, 0.0)
                total = total + weight * products[s, part * SHARE:(part + 1) * SHARE]
            partial[b, part] = total
        pair(b).start()
        if place:
            finish(order[place - 1])
    finish(0)
    for k in (1, 2, 3):
        to_y(k).wait_recv()
    own = half[y] + received2[0] + received2[1] + received2[2]
    own_ref[...] = own
    gram[...] = lax.dot_general(
        own, own, (((0,), (0,)), ((), ())), precision=HIGHEST, preferred_element_type=jnp.float32
    ).reshape(GROUP, 8, WIDTH)

    def scatter(k):
        other, row, col = member(k)
        return copy_to(gram.at[other], slots.at[k - 1], g_send.at[k - 1], g_recv.at[k - 1], row, col)

    def near(k, source):
        piece = lows.at[source]
        return copy_to(piece, piece, l_send.at[k - 1], l_recv.at[k - 1], at_low(k), c)

    def far(k, source):
        piece = highs.at[source]
        return copy_to(piece, piece, h_send.at[k - 1], h_recv.at[k - 1], at_high(k), c)

    def spread(k, source):
        _, row, col = member(k)
        piece = gram_ref.at[source]
        return copy_to(piece, piece, s_send.at[k - 1], s_recv.at[k - 1], row, col)

    def each(stop, act):
        def body(k, carry):
            act(k)
            return carry
        lax.fori_loop(1, stop, body, 0)

    each(GROUP, lambda k: scatter(k).start())
    each(GROUP, lambda k: scatter(k).wait_recv())
    lows[low] = gram[me] + jnp.sum(slots[...], axis=0)
    each(LINE, lambda k: near(k, low).start())
    each(LINE, lambda k: near(k, lax.rem(low + LINE - k, LINE)).wait_recv())
    highs[high] = jnp.sum(lows[...], axis=0)
    each(LINE, lambda k: far(k, high).start())
    each(LINE, lambda k: far(k, lax.rem(high + LINE - k, LINE)).wait_recv())
    gram_ref[me] = jnp.sum(highs[...], axis=0)
    each(GROUP, lambda k: spread(k, me).start())
    for k in range(NY):
        pair(k).wait_send()
    for k in (1, 2, 3):
        to_y(k).wait_send()
    each(GROUP, lambda k: scatter(k).wait_send())
    each(LINE, lambda k: near(k, low).wait_send())
    each(LINE, lambda k: far(k, high).wait_send())
    each(GROUP, lambda k: spread(k, lax.rem(me + GROUP - k, GROUP)).wait_recv())
    each(GROUP, lambda k: spread(k, me).wait_send())


def factor_kernel(step, root, gram_ref, own_ref, basis_ref, factor_ref, work, rows):
    f32 = jnp.float32
    lane = lax.broadcasted_iota(jnp.int32, (1, HALF), 1)
    below = lax.broadcasted_iota(jnp.int32, (HALF, HALF), 0) > lax.broadcasted_iota(
        jnp.int32, (HALF, HALF), 1
    )
    eye = (
        lax.broadcasted_iota(jnp.int32, (HALF, HALF), 0)
        == lax.broadcasted_iota(jnp.int32, (HALF, HALF), 1)
    ).astype(f32)

    def dot(a, b, dims):
        return lax.dot_general(a, b, (dims, ((), ())), precision=HIGHEST, preferred_element_type=f32)

    def pick(value, j):
        return jnp.sum(jnp.where(lane == j, value, 0.0), axis=1, keepdims=True)

    def eliminate(block):
        work[:, :HALF] = block
        work[:, HALF:] = eye

        def body(i, carry):
            j = i * step
            line = [work[pl.ds(j + t, 1), :] for t in range(step)]
            column = [pick(work[:, :HALF], j + t) for t in range(step)]
            entry = [[pick(line[t][:, :HALF], j + u) for u in range(step)] for t in range(step)]
            scaled = []
            for t in range(step):
                inverse = 1.0 / entry[t][t]
                for u in range(t + 1, step):
                    ratio = entry[t][u] * inverse
                    line[u] = line[u] - ratio * line[t]
                    column[u] = column[u] - ratio * column[t]
                    for v in range(u, step):
                        entry[u][v] = entry[u][v] - ratio * entry[t][v]
                scaled.append(line[t] * inverse)
            total = work[...]
            for t in range(step):
                total = total - column[t] * scaled[t]
            work[...] = total
            for t in range(step):
                rows[pl.ds(j + t, 1), :] = line[t] * (1.0 / jnp.sqrt(entry[t][t]))
            return carry

        lax.fori_loop(0, HALF // step, body, 0)
        return jnp.where(below, 0.0, rows[:, :HALF]), rows[:, HALF:]

    upper1, inverse1 = eliminate(gram_ref[:HALF, :HALF])
    cross = dot(inverse1, gram_ref[:HALF, HALF:], ((1,), (0,)))
    factor_ref[:HALF, :HALF] = upper1 * (1.0 / root)
    factor_ref[:HALF, HALF:] = cross * (1.0 / root)
    factor_ref[HALF:, :HALF] = jnp.zeros((HALF, HALF), f32)
    solved = dot(own_ref[:, :HALF], inverse1, ((1,), (1,)))
    basis_ref[:, :HALF] = solved * root
    rest = own_ref[:, HALF:] - dot(solved, cross, ((1,), (0,)))
    schur = gram_ref[HALF:, HALF:] - dot(cross, cross, ((0,), (0,)))
    upper2, inverse2 = eliminate(schur)
    factor_ref[HALF:, HALF:] = upper2 * (1.0 / root)
    basis_ref[:, HALF:] = dot(rest, inverse2, ((1,), (1,))) * root


def factorize(gram, own, step):
    root = float(RB * WIDTH * NX * NZ) ** 0.5
    f32 = jnp.float32
    vmem = pl.BlockSpec(memory_space=pltpu.VMEM)
    return pl.pallas_call(
        functools.partial(factor_kernel, step, root),
        out_shape=(
            jax.ShapeDtypeStruct((SHARE, WIDTH), f32),
            jax.ShapeDtypeStruct((WIDTH, WIDTH), f32),
        ),
        in_specs=[vmem, vmem],
        out_specs=(vmem, vmem),
        scratch_shapes=[pltpu.VMEM((HALF, WIDTH), f32), pltpu.VMEM((HALF, WIDTH), f32)],
        name="factorize",
    )(gram, own)


def local(sketch, blocks, block_rows, block_cols, counts):
    f32 = jnp.float32
    dma = pltpu.SemaphoreType.DMA
    vmem = pl.BlockSpec(memory_space=pltpu.VMEM)
    smem = pl.BlockSpec(memory_space=pltpu.SMEM)
    own, gram = pl.pallas_call(
        sketch_kernel,
        out_shape=(
            jax.ShapeDtypeStruct((SHARE, WIDTH), f32),
            jax.ShapeDtypeStruct((GROUP, 8, WIDTH), f32),
        ),
        in_specs=[smem, smem, smem, vmem, vmem],
        out_specs=(vmem, vmem),
        scratch_shapes=[
            pltpu.VMEM((NX, NZ, WIDTH, WIDTH), jnp.bfloat16),
            pltpu.VMEM((8, WIDTH, WIDTH), f32),
            pltpu.VMEM((RB, NC, SHARE, WIDTH), f32),
            pltpu.VMEM((RB, SHARE, WIDTH), f32),
            pltpu.VMEM((RB, SHARE, WIDTH), f32),
            pltpu.VMEM((NY - 1, SHARE, WIDTH), f32),
            pltpu.VMEM((GROUP, 8, WIDTH), f32),
            pltpu.VMEM((GROUP - 1, 8, WIDTH), f32),
            pltpu.VMEM((LINE, 8, WIDTH), f32),
            pltpu.VMEM((LINE, 8, WIDTH), f32),
            dma,
            dma((3,)), dma((3,)),
            dma((2, 8)), dma((2, 8)),
            dma((2, 8)), dma((2, 8)),
            dma((2, 2, 8)), dma((2, 2, 8)),
            dma((2, 8)), dma((2, 8)),
            dma((4,)), dma((4,)),
            dma((3,)), dma((3,)),
            dma((GROUP - 1,)), dma((GROUP - 1,)),
            dma((3,)), dma((3,)),
            dma((3,)), dma((3,)),
            dma((GROUP - 1,)), dma((GROUP - 1,)),
        ],
        compiler_params=pltpu.CompilerParams(collective_id=0, has_side_effects=True),
        name="sketch",
    )(block_rows, block_cols, counts, sketch, blocks)
    gram = gram.reshape(WIDTH, WIDTH)
    return factorize(gram, own, 4)


def solution(mesh):
    in_specs = (
        P(("rows", "cols"), None),
        P(("rows", "cols"), None, None),
        P(("rows", "cols")),
        P(("rows", "cols")),
        P(("rows", "cols")),
    )
    out_specs = (P(("rows", "cols"), None), P())
    return jax.shard_map(local, mesh=mesh, in_specs=in_specs, out_specs=out_specs, check_vma=False)
```

```python
import functools

import jax
import jax.numpy as jnp
from jax import lax
from jax.experimental import pallas as pl
from jax.experimental.pallas import tpu as pltpu
from jax.sharding import PartitionSpec as P

MESH = pl.DeviceIdType.MESH
HIGHEST = lax.Precision.HIGHEST
RB = 4
NX, NZ, NY, NC = 4, 16, 4, 2
WIDTH = 256
SPLIT = 80
GROUP = 32
SHARE = 128
HALF = 128


def copy_to(src, dst, send_sem, recv_sem, row, col):
    return pltpu.make_async_remote_copy(
        src_ref=src, dst_ref=dst, send_sem=send_sem, recv_sem=recv_sem,
        device_id=(row, col), device_id_type=MESH,
    )


def sketch_kernel(
    rows_ref, cols_ref, counts_ref, sketch_ref, blocks_ref, own_ref, gram_ref,
    panel, products, partial, received, half, received2, gram, slots, lows,
    local_sem, xa_send, xa_recv, za_send, za_recv, zb_send, zb_recv,
    xb_send, xb_recv, op_send, op_recv, c_send, c_recv, y_send, y_recv,
    g_send, g_recv, l_send, l_recv, s_send, s_recv,
):
    r = lax.axis_index("rows")
    c = lax.axis_index("cols")
    x, z = r // NZ, lax.rem(r, NZ)
    y, core = c // NC, lax.rem(c, NC)

    def at_x(k):
        return lax.rem(x + k, NX) * NZ + z

    def at_z(k):
        return x * NZ + lax.rem(z + k, NZ)

    cols = NY * NC
    me = x * cols + c

    def member(k):
        other = lax.rem(me + k, GROUP)
        return other, (other // cols) * NZ + z, lax.rem(other, cols)

    barrier = pltpu.get_barrier_semaphore()

    def hello(row, col):
        pl.semaphore_signal(barrier, inc=1, device_id=(row, col), device_id_type=MESH)

    for row in (at_z(1), at_z(NZ - 1), at_x(1), at_x(2), at_x(3)):
        hello(row, c)
    hello(r, y * NC + 1 - core)
    for k in (1, 2, 3):
        hello(r, lax.rem(y + k, NY) * NC + core)
    pl.semaphore_wait(barrier, 9)

    local = pltpu.make_async_copy(sketch_ref, panel.at[x, z], local_sem)
    local.start()

    first = pl.ds(0, SPLIT)
    second = pl.ds(SPLIT, WIDTH - SPLIT)

    def shifted(k):
        return lax.rem(z + k + NZ, NZ)

    def xa(k):
        piece = panel.at[x, z, first]
        return copy_to(sketch_ref.at[first], piece, xa_send.at[k - 1], xa_recv.at[k - 1], at_x(k), c)

    def za(side, hop):
        step = 1 - 2 * side
        piece = panel.at[:, shifted(-step * (hop - 1)), first]
        to = at_z(1 if side == 0 else NZ - 1)
        return copy_to(piece, piece, za_send.at[side, hop - 1], za_recv.at[side, hop - 1], to, c)

    def za_arrived(side, hop):
        step = 1 - 2 * side
        piece = panel.at[:, shifted(-step * hop), first]
        to = at_z(1 if side == 0 else NZ - 1)
        copy_to(piece, piece, za_send.at[side, hop - 1], za_recv.at[side, hop - 1], to, c).wait_recv()

    def zb(side, hop):
        step = 1 - 2 * side
        piece = panel.at[x, shifted(-step * (hop - 1)), second]
        to = at_z(1 if side == 0 else NZ - 1)
        return copy_to(piece, piece, zb_send.at[side, hop - 1], zb_recv.at[side, hop - 1], to, c)

    def zb_arrived(side, hop):
        step = 1 - 2 * side
        piece = panel.at[x, shifted(-step * hop), second]
        to = at_z(1 if side == 0 else NZ - 1)
        copy_to(piece, piece, zb_send.at[side, hop - 1], zb_recv.at[side, hop - 1], to, c).wait_recv()

    def piece_of(family, slot, column):
        at = shifted(-slot - 1) if family == 0 else shifted(slot)
        return panel.at[column, at, second]

    def xb(family, slot, way):
        piece = piece_of(family, slot, x)
        to = at_x(1 if way == 0 else NX - 1)
        return copy_to(piece, piece, xb_send.at[family, way, slot], xb_recv.at[family, way, slot], to, c)

    def xb_arrived(family, slot, way):
        column = lax.rem(x + (NX - 1 if way == 0 else 1), NX)
        piece = piece_of(family, slot, column)
        to = at_x(1 if way == 0 else NX - 1)
        copy_to(piece, piece, xb_send.at[family, way, slot], xb_recv.at[family, way, slot], to, c).wait_recv()

    def op(family, slot):
        column = lax.rem(x + (NX - 1 if family == 0 else 1), NX)
        piece = piece_of(family, slot, column)
        to = at_x(1 if family == 0 else NX - 1)
        return copy_to(piece, piece, op_send.at[family, slot], op_recv.at[family, slot], to, c)

    def op_arrived(family, slot):
        piece = piece_of(family, slot, lax.rem(x + 2, NX))
        to = at_x(1 if family == 0 else NX - 1)
        copy_to(piece, piece, op_send.at[family, slot], op_recv.at[family, slot], to, c).wait_recv()

    for k in (1, 2, 3):
        xa(k).start()
    local.wait()
    for side in (0, 1):
        zb(side, 1).start()
    for way in (0, 1):
        xb(1, 0, way).start()
    for k in (1, 2, 3):
        piece = panel.at[lax.rem(x + NX - k, NX), z, first]
        copy_to(piece, piece, xa_send.at[k - 1], xa_recv.at[k - 1], at_x(k), c).wait_recv()
    for side in (0, 1):
        za(side, 1).start()

    def hop_body(hop, carry):
        zb_arrived(0, hop)
        zb(0, hop + 1).start()
        for way in (0, 1):
            xb(0, hop - 1, way).start()
        zb_arrived(1, hop)

        @pl.when(hop < 7)
        def _():
            zb(1, hop + 1).start()

        for way in (0, 1):
            xb(1, hop, way).start()
        za_arrived(1, hop)
        za(1, hop + 1).start()
        za_arrived(0, hop)

        @pl.when(hop < 7)
        def _():
            za(0, hop + 1).start()

        xb_arrived(1, hop - 1, 1)
        op(1, hop - 1).start()

        @pl.when(hop > 1)
        def _():
            xb_arrived(0, hop - 2, 0)
            op(0, hop - 2).start()

        return carry

    lax.fori_loop(1, 8, hop_body, 0)
    zb_arrived(0, 8)
    for way in (0, 1):
        xb(0, 7, way).start()
    xb_arrived(1, 7, 1)
    op(1, 7).start()
    xb_arrived(0, 6, 0)
    op(0, 6).start()
    xb_arrived(0, 7, 0)
    op(0, 7).start()
    za_arrived(1, 8)

    def drain(slot, carry):
        xb_arrived(0, slot, 1)
        xb_arrived(1, slot, 0)
        for family in (0, 1):
            op_arrived(family, slot)
            op(family, slot).wait_send()
            for way in (0, 1):
                xb(family, slot, way).wait_send()
        zb(0, slot + 1).wait_send()
        za(1, slot + 1).wait_send()

        @pl.when(slot < 7)
        def _():
            zb(1, slot + 1).wait_send()
            za(0, slot + 1).wait_send()

        return carry

    lax.fori_loop(0, 8, drain, 0)
    for k in (1, 2, 3):
        xa(k).wait_send()

    live = counts_ref[0]

    def slot_body(s, carry):
        q = cols_ref[s]
        products[s] = jnp.dot(
            blocks_ref[s], panel[q // NZ, lax.rem(q, NZ)], preferred_element_type=jnp.float32
        )
        return carry

    lax.fori_loop(0, 8, slot_body, 0)

    def pair(b):
        return copy_to(
            partial.at[b, 1 - core], received.at[b], c_send.at[b], c_recv.at[b], r, y * NC + 1 - core
        )

    def to_y(k):
        other = lax.rem(y + k, NY)
        return copy_to(
            half.at[other], received2.at[k - 1], y_send.at[k - 1], y_recv.at[k - 1], r, other * NC + core
        )

    def finish(k):
        b = lax.rem(y + k, NY)
        pair(b).wait_recv()
        half[b] = partial[b, core] + received[b]
        if k:
            to_y(k).start()

    order = (2, 1, 3, 0)
    for place, k in enumerate(order):
        b = lax.rem(y + k, NY)
        for part in range(NC):
            total = jnp.zeros((SHARE, WIDTH), jnp.float32)
            for s in range(8):
                weight = jnp.where(jnp.logical_and(rows_ref[s] == b, s < live), 1.0, 0.0)
                total = total + weight * products[s, part * SHARE:(part + 1) * SHARE]
            partial[b, part] = total
        pair(b).start()
        if place:
            finish(order[place - 1])
    finish(0)
    for k in (1, 2, 3):
        to_y(k).wait_recv()
    own = half[y] + received2[0] + received2[1] + received2[2]
    own_ref[...] = own
    gram[...] = lax.dot_general(
        own, own, (((0,), (0,)), ((), ())), precision=HIGHEST, preferred_element_type=jnp.float32
    ).reshape(GROUP, 8, WIDTH)

    def scatter(k):
        other, row, col = member(k)
        return copy_to(gram.at[other], slots.at[k - 1], g_send.at[k - 1], g_recv.at[k - 1], row, col)

    def line(i, source):
        hops = 8 - i // 2
        k = lax.rem(i, 2) * (NZ - 2 * hops) + hops
        return copy_to(lows.at[source(k)], lows.at[source(k)], l_send.at[i], l_recv.at[i], at_z(k), c)

    def spread(k, source):
        _, row, col = member(k)
        piece = gram_ref.at[source]
        return copy_to(piece, piece, s_send.at[k - 1], s_recv.at[k - 1], row, col)

    def each(stop, act):
        def body(k, carry):
            act(k)
            return carry
        lax.fori_loop(1, stop, body, 0)

    each(GROUP, lambda k: scatter(k).start())
    each(GROUP, lambda k: scatter(k).wait_recv())
    def along(act):
        def body(i, carry):
            act(i)
            return carry
        lax.fori_loop(1, NZ, body, 0)

    lows[z] = gram[me] + jnp.sum(slots[...], axis=0)
    along(lambda i: line(i, lambda k: z).start())
    along(lambda i: line(i, lambda k: lax.rem(z + NZ - k, NZ)).wait_recv())
    gram_ref[me] = jnp.sum(lows[...], axis=0)
    each(GROUP, lambda k: spread(k, me).start())
    for k in range(NY):
        pair(k).wait_send()
    for k in (1, 2, 3):
        to_y(k).wait_send()
    each(GROUP, lambda k: scatter(k).wait_send())
    along(lambda i: line(i, lambda k: z).wait_send())
    each(GROUP, lambda k: spread(k, lax.rem(me + GROUP - k, GROUP)).wait_recv())
    each(GROUP, lambda k: spread(k, me).wait_send())


def factor_kernel(step, root, gram_ref, own_ref, basis_ref, factor_ref, work, rows):
    f32 = jnp.float32
    lane = lax.broadcasted_iota(jnp.int32, (1, HALF), 1)
    below = lax.broadcasted_iota(jnp.int32, (HALF, HALF), 0) > lax.broadcasted_iota(
        jnp.int32, (HALF, HALF), 1
    )
    eye = (
        lax.broadcasted_iota(jnp.int32, (HALF, HALF), 0)
        == lax.broadcasted_iota(jnp.int32, (HALF, HALF), 1)
    ).astype(f32)

    def dot(a, b, dims):
        return lax.dot_general(a, b, (dims, ((), ())), precision=HIGHEST, preferred_element_type=f32)

    def pick(value, j):
        return jnp.sum(jnp.where(lane == j, value, 0.0), axis=1, keepdims=True)

    def eliminate(block):
        work[:, :HALF] = block
        work[:, HALF:] = eye

        def body(i, carry):
            j = i * step
            line = [work[pl.ds(j + t, 1), :] for t in range(step)]
            column = [pick(work[:, :HALF], j + t) for t in range(step)]
            entry = [[pick(line[t][:, :HALF], j + u) for u in range(step)] for t in range(step)]
            scaled = []
            for t in range(step):
                inverse = 1.0 / entry[t][t]
                for u in range(t + 1, step):
                    ratio = entry[t][u] * inverse
                    line[u] = line[u] - ratio * line[t]
                    column[u] = column[u] - ratio * column[t]
                    for v in range(u, step):
                        entry[u][v] = entry[u][v] - ratio * entry[t][v]
                scaled.append(line[t] * inverse)
            total = work[...]
            for t in range(step):
                total = total - column[t] * scaled[t]
            work[...] = total
            for t in range(step):
                rows[pl.ds(j + t, 1), :] = line[t] * (1.0 / jnp.sqrt(entry[t][t]))
            return carry

        lax.fori_loop(0, HALF // step, body, 0)
        return jnp.where(below, 0.0, rows[:, :HALF]), rows[:, HALF:]

    upper1, inverse1 = eliminate(gram_ref[:HALF, :HALF])
    cross = dot(inverse1, gram_ref[:HALF, HALF:], ((1,), (0,)))
    factor_ref[:HALF, :HALF] = upper1 * (1.0 / root)
    factor_ref[:HALF, HALF:] = cross * (1.0 / root)
    factor_ref[HALF:, :HALF] = jnp.zeros((HALF, HALF), f32)
    solved = dot(own_ref[:, :HALF], inverse1, ((1,), (1,)))
    basis_ref[:, :HALF] = solved * root
    rest = own_ref[:, HALF:] - dot(solved, cross, ((1,), (0,)))
    schur = gram_ref[HALF:, HALF:] - dot(cross, cross, ((0,), (0,)))
    upper2, inverse2 = eliminate(schur)
    factor_ref[HALF:, HALF:] = upper2 * (1.0 / root)
    basis_ref[:, HALF:] = dot(rest, inverse2, ((1,), (1,))) * root


def factorize(gram, own, step):
    root = float(RB * WIDTH * NX * NZ) ** 0.5
    f32 = jnp.float32
    vmem = pl.BlockSpec(memory_space=pltpu.VMEM)
    return pl.pallas_call(
        functools.partial(factor_kernel, step, root),
        out_shape=(
            jax.ShapeDtypeStruct((SHARE, WIDTH), f32),
            jax.ShapeDtypeStruct((WIDTH, WIDTH), f32),
        ),
        in_specs=[vmem, vmem],
        out_specs=(vmem, vmem),
        scratch_shapes=[pltpu.VMEM((HALF, WIDTH), f32), pltpu.VMEM((HALF, WIDTH), f32)],
        name="factorize",
    )(gram, own)


def local(sketch, blocks, block_rows, block_cols, counts):
    f32 = jnp.float32
    dma = pltpu.SemaphoreType.DMA
    vmem = pl.BlockSpec(memory_space=pltpu.VMEM)
    smem = pl.BlockSpec(memory_space=pltpu.SMEM)
    own, gram = pl.pallas_call(
        sketch_kernel,
        out_shape=(
            jax.ShapeDtypeStruct((SHARE, WIDTH), f32),
            jax.ShapeDtypeStruct((GROUP, 8, WIDTH), f32),
        ),
        in_specs=[smem, smem, smem, vmem, vmem],
        out_specs=(vmem, vmem),
        scratch_shapes=[
            pltpu.VMEM((NX, NZ, WIDTH, WIDTH), jnp.bfloat16),
            pltpu.VMEM((8, WIDTH, WIDTH), f32),
            pltpu.VMEM((RB, NC, SHARE, WIDTH), f32),
            pltpu.VMEM((RB, SHARE, WIDTH), f32),
            pltpu.VMEM((RB, SHARE, WIDTH), f32),
            pltpu.VMEM((NY - 1, SHARE, WIDTH), f32),
            pltpu.VMEM((GROUP, 8, WIDTH), f32),
            pltpu.VMEM((GROUP - 1, 8, WIDTH), f32),
            pltpu.VMEM((NZ, 8, WIDTH), f32),
            dma,
            dma((3,)), dma((3,)),
            dma((2, 8)), dma((2, 8)),
            dma((2, 8)), dma((2, 8)),
            dma((2, 2, 8)), dma((2, 2, 8)),
            dma((2, 8)), dma((2, 8)),
            dma((4,)), dma((4,)),
            dma((3,)), dma((3,)),
            dma((GROUP - 1,)), dma((GROUP - 1,)),
            dma((NZ,)), dma((NZ,)),
            dma((GROUP - 1,)), dma((GROUP - 1,)),
        ],
        compiler_params=pltpu.CompilerParams(collective_id=0, has_side_effects=True),
        name="sketch",
    )(block_rows, block_cols, counts, sketch, blocks)
    gram = gram.reshape(WIDTH, WIDTH)
    return factorize(gram, own, 4)


def solution(mesh):
    in_specs = (
        P(("rows", "cols"), None),
        P(("rows", "cols"), None, None),
        P(("rows", "cols")),
        P(("rows", "cols")),
        P(("rows", "cols")),
    )
    out_specs = (P(("rows", "cols"), None), P())
    return jax.shard_map(local, mesh=mesh, in_specs=in_specs, out_specs=out_specs, check_vma=False)
```

```python
import functools

import jax
import jax.numpy as jnp
from jax import lax
from jax.experimental import pallas as pl
from jax.experimental.pallas import tpu as pltpu
from jax.sharding import PartitionSpec as P

MESH = pl.DeviceIdType.MESH
HIGHEST = lax.Precision.HIGHEST
RB = 4
NX, NZ, NY, NC = 4, 16, 4, 2
WIDTH = 256
SPLIT = 80
GROUP = 32
SHARE = 128
BLOCK = 64


def copy_to(src, dst, send_sem, recv_sem, row, col):
    return pltpu.make_async_remote_copy(
        src_ref=src, dst_ref=dst, send_sem=send_sem, recv_sem=recv_sem,
        device_id=(row, col), device_id_type=MESH,
    )


def sketch_kernel(
    rows_ref, cols_ref, counts_ref, sketch_ref, blocks_ref, own_ref, gram_ref,
    panel, products, partial, received, half, received2, gram, slots, lows,
    local_sem, xa_send, xa_recv, za_send, za_recv, zb_send, zb_recv,
    xb_send, xb_recv, op_send, op_recv, c_send, c_recv, y_send, y_recv,
    g_send, g_recv, l_send, l_recv, s_send, s_recv,
):
    r = lax.axis_index("rows")
    c = lax.axis_index("cols")
    x, z = r // NZ, lax.rem(r, NZ)
    y, core = c // NC, lax.rem(c, NC)

    def at_x(k):
        return lax.rem(x + k, NX) * NZ + z

    def at_z(k):
        return x * NZ + lax.rem(z + k, NZ)

    cols = NY * NC
    me = x * cols + c

    def member(k):
        other = lax.rem(me + k, GROUP)
        return other, (other // cols) * NZ + z, lax.rem(other, cols)

    barrier = pltpu.get_barrier_semaphore()

    def hello(row, col):
        pl.semaphore_signal(barrier, inc=1, device_id=(row, col), device_id_type=MESH)

    for row in (at_z(1), at_z(NZ - 1), at_x(1), at_x(2), at_x(3)):
        hello(row, c)
    hello(r, y * NC + 1 - core)
    for k in (1, 2, 3):
        hello(r, lax.rem(y + k, NY) * NC + core)
    pl.semaphore_wait(barrier, 9)

    local = pltpu.make_async_copy(sketch_ref, panel.at[x, z], local_sem)
    local.start()

    first = pl.ds(0, SPLIT)
    second = pl.ds(SPLIT, WIDTH - SPLIT)

    def shifted(k):
        return lax.rem(z + k + NZ, NZ)

    def xa(k):
        piece = panel.at[x, z, first]
        return copy_to(sketch_ref.at[first], piece, xa_send.at[k - 1], xa_recv.at[k - 1], at_x(k), c)

    def za(side, hop):
        step = 1 - 2 * side
        piece = panel.at[:, shifted(-step * (hop - 1)), first]
        to = at_z(1 if side == 0 else NZ - 1)
        return copy_to(piece, piece, za_send.at[side, hop - 1], za_recv.at[side, hop - 1], to, c)

    def za_arrived(side, hop):
        step = 1 - 2 * side
        piece = panel.at[:, shifted(-step * hop), first]
        to = at_z(1 if side == 0 else NZ - 1)
        copy_to(piece, piece, za_send.at[side, hop - 1], za_recv.at[side, hop - 1], to, c).wait_recv()

    def zb(side, hop):
        step = 1 - 2 * side
        piece = panel.at[x, shifted(-step * (hop - 1)), second]
        to = at_z(1 if side == 0 else NZ - 1)
        return copy_to(piece, piece, zb_send.at[side, hop - 1], zb_recv.at[side, hop - 1], to, c)

    def zb_arrived(side, hop):
        step = 1 - 2 * side
        piece = panel.at[x, shifted(-step * hop), second]
        to = at_z(1 if side == 0 else NZ - 1)
        copy_to(piece, piece, zb_send.at[side, hop - 1], zb_recv.at[side, hop - 1], to, c).wait_recv()

    def piece_of(family, slot, column):
        at = shifted(-slot - 1) if family == 0 else shifted(slot)
        return panel.at[column, at, second]

    def xb(family, slot, way):
        piece = piece_of(family, slot, x)
        to = at_x(1 if way == 0 else NX - 1)
        return copy_to(piece, piece, xb_send.at[family, way, slot], xb_recv.at[family, way, slot], to, c)

    def xb_arrived(family, slot, way):
        column = lax.rem(x + (NX - 1 if way == 0 else 1), NX)
        piece = piece_of(family, slot, column)
        to = at_x(1 if way == 0 else NX - 1)
        copy_to(piece, piece, xb_send.at[family, way, slot], xb_recv.at[family, way, slot], to, c).wait_recv()

    def op(family, slot):
        column = lax.rem(x + (NX - 1 if family == 0 else 1), NX)
        piece = piece_of(family, slot, column)
        to = at_x(1 if family == 0 else NX - 1)
        return copy_to(piece, piece, op_send.at[family, slot], op_recv.at[family, slot], to, c)

    def op_arrived(family, slot):
        piece = piece_of(family, slot, lax.rem(x + 2, NX))
        to = at_x(1 if family == 0 else NX - 1)
        copy_to(piece, piece, op_send.at[family, slot], op_recv.at[family, slot], to, c).wait_recv()

    for k in (1, 2, 3):
        xa(k).start()
    local.wait()
    for side in (0, 1):
        zb(side, 1).start()
    for way in (0, 1):
        xb(1, 0, way).start()
    for k in (1, 2, 3):
        piece = panel.at[lax.rem(x + NX - k, NX), z, first]
        copy_to(piece, piece, xa_send.at[k - 1], xa_recv.at[k - 1], at_x(k), c).wait_recv()
    for side in (0, 1):
        za(side, 1).start()

    def hop_body(hop, carry):
        zb_arrived(0, hop)
        zb(0, hop + 1).start()
        for way in (0, 1):
            xb(0, hop - 1, way).start()
        zb_arrived(1, hop)

        @pl.when(hop < 7)
        def _():
            zb(1, hop + 1).start()

        for way in (0, 1):
            xb(1, hop, way).start()
        za_arrived(1, hop)
        za(1, hop + 1).start()
        za_arrived(0, hop)

        @pl.when(hop < 7)
        def _():
            za(0, hop + 1).start()

        xb_arrived(1, hop - 1, 1)
        op(1, hop - 1).start()

        @pl.when(hop > 1)
        def _():
            xb_arrived(0, hop - 2, 0)
            op(0, hop - 2).start()

        return carry

    lax.fori_loop(1, 8, hop_body, 0)
    zb_arrived(0, 8)
    for way in (0, 1):
        xb(0, 7, way).start()
    xb_arrived(1, 7, 1)
    op(1, 7).start()
    xb_arrived(0, 6, 0)
    op(0, 6).start()
    xb_arrived(0, 7, 0)
    op(0, 7).start()
    za_arrived(1, 8)

    def drain(slot, carry):
        xb_arrived(0, slot, 1)
        xb_arrived(1, slot, 0)
        for family in (0, 1):
            op_arrived(family, slot)
            op(family, slot).wait_send()
            for way in (0, 1):
                xb(family, slot, way).wait_send()
        zb(0, slot + 1).wait_send()
        za(1, slot + 1).wait_send()

        @pl.when(slot < 7)
        def _():
            zb(1, slot + 1).wait_send()
            za(0, slot + 1).wait_send()

        return carry

    lax.fori_loop(0, 8, drain, 0)
    for k in (1, 2, 3):
        xa(k).wait_send()

    live = counts_ref[0]

    def slot_body(s, carry):
        q = cols_ref[s]
        products[s] = jnp.dot(
            blocks_ref[s], panel[q // NZ, lax.rem(q, NZ)], preferred_element_type=jnp.float32
        )
        return carry

    lax.fori_loop(0, 8, slot_body, 0)

    def pair(b):
        return copy_to(
            partial.at[b, 1 - core], received.at[b], c_send.at[b], c_recv.at[b], r, y * NC + 1 - core
        )

    def to_y(k):
        other = lax.rem(y + k, NY)
        return copy_to(
            half.at[other], received2.at[k - 1], y_send.at[k - 1], y_recv.at[k - 1], r, other * NC + core
        )

    def finish(k):
        b = lax.rem(y + k, NY)
        pair(b).wait_recv()
        half[b] = partial[b, core] + received[b]
        if k:
            to_y(k).start()

    order = (2, 1, 3, 0)
    for place, k in enumerate(order):
        b = lax.rem(y + k, NY)
        for part in range(NC):
            total = jnp.zeros((SHARE, WIDTH), jnp.float32)
            for s in range(8):
                weight = jnp.where(jnp.logical_and(rows_ref[s] == b, s < live), 1.0, 0.0)
                total = total + weight * products[s, part * SHARE:(part + 1) * SHARE]
            partial[b, part] = total
        pair(b).start()
        if place:
            finish(order[place - 1])
    finish(0)
    for k in (1, 2, 3):
        to_y(k).wait_recv()
    own = half[y] + received2[0] + received2[1] + received2[2]
    own_ref[...] = own
    gram[...] = lax.dot_general(
        own, own, (((0,), (0,)), ((), ())), precision=HIGHEST, preferred_element_type=jnp.float32
    ).reshape(GROUP, 8, WIDTH)

    def scatter(k):
        other, row, col = member(k)
        return copy_to(gram.at[other], slots.at[k - 1], g_send.at[k - 1], g_recv.at[k - 1], row, col)

    def line(i, source):
        hops = 8 - i // 2
        k = lax.rem(i, 2) * (NZ - 2 * hops) + hops
        return copy_to(lows.at[source(k)], lows.at[source(k)], l_send.at[i], l_recv.at[i], at_z(k), c)

    def spread(k, source):
        _, row, col = member(k)
        piece = gram_ref.at[source]
        return copy_to(piece, piece, s_send.at[k - 1], s_recv.at[k - 1], row, col)

    def each(stop, act):
        def body(k, carry):
            act(k)
            return carry
        lax.fori_loop(1, stop, body, 0)

    each(GROUP, lambda k: scatter(k).start())
    each(GROUP, lambda k: scatter(k).wait_recv())
    def along(act):
        def body(i, carry):
            act(i)
            return carry
        lax.fori_loop(1, NZ, body, 0)

    lows[z] = gram[me] + jnp.sum(slots[...], axis=0)
    along(lambda i: line(i, lambda k: z).start())
    along(lambda i: line(i, lambda k: lax.rem(z + NZ - k, NZ)).wait_recv())
    gram_ref[me] = jnp.sum(lows[...], axis=0)
    each(GROUP, lambda k: spread(k, me).start())
    for k in range(NY):
        pair(k).wait_send()
    for k in (1, 2, 3):
        to_y(k).wait_send()
    each(GROUP, lambda k: scatter(k).wait_send())
    along(lambda i: line(i, lambda k: z).wait_send())
    each(GROUP, lambda k: spread(k, lax.rem(me + GROUP - k, GROUP)).wait_recv())
    each(GROUP, lambda k: spread(k, me).wait_send())


def factor_kernel(step, root, gram_ref, own_ref, basis_ref, factor_ref, work, rows):
    f32 = jnp.float32
    lane = lax.broadcasted_iota(jnp.int32, (1, 2 * BLOCK), 1)
    row_index = lax.broadcasted_iota(jnp.int32, (BLOCK, BLOCK), 0)
    lane_index = lax.broadcasted_iota(jnp.int32, (BLOCK, BLOCK), 1)
    below = row_index > lane_index
    eye = (row_index == lane_index).astype(f32)

    def dot(a, b, dims):
        return lax.dot_general(a, b, (dims, ((), ())), precision=HIGHEST, preferred_element_type=f32)

    def pick(value, j):
        return jnp.sum(jnp.where(lane == j, value, 0.0), axis=1, keepdims=True)

    def eliminate(block):
        work[...] = jnp.concatenate([block, eye], axis=1)

        def body(i, carry):
            j = i * step
            line = [work[pl.ds(j + t, 1), :] for t in range(step)]
            column = [pick(work[...], j + t) for t in range(step)]
            entry = [[pick(line[t], j + u) for u in range(step)] for t in range(step)]
            scaled = []
            for t in range(step):
                inverse = 1.0 / entry[t][t]
                for u in range(t + 1, step):
                    ratio = entry[t][u] * inverse
                    line[u] = line[u] - ratio * line[t]
                    column[u] = column[u] - ratio * column[t]
                    for v in range(u, step):
                        entry[u][v] = entry[u][v] - ratio * entry[t][v]
                scaled.append(line[t] * inverse)
            total = work[...]
            for t in range(step):
                total = total - column[t] * scaled[t]
            work[...] = total
            for t in range(step):
                rows[pl.ds(j + t, 1), :] = line[t] * (1.0 / jnp.sqrt(entry[t][t]))
            return carry

        lax.fori_loop(0, BLOCK // step, body, 0)
        return jnp.where(below, 0.0, rows[:, :BLOCK]), rows[:, BLOCK:]

    rest, share = gram_ref[...], own_ref[...]
    for first in range(0, WIDTH, BLOCK):
        last = first + BLOCK
        upper, inverse = eliminate(rest[:BLOCK, :BLOCK])
        factor_ref[first:last, first:last] = upper * (1.0 / root)
        if first:
            factor_ref[first:last, :first] = jnp.zeros((BLOCK, first), f32)
        solved = dot(share[:, :BLOCK], inverse, ((1,), (1,)))
        basis_ref[:, first:last] = solved * root
        if last < WIDTH:
            cross = dot(inverse, rest[:BLOCK, BLOCK:], ((1,), (0,)))
            factor_ref[first:last, last:] = cross * (1.0 / root)
            share = share[:, BLOCK:] - dot(solved, cross, ((1,), (0,)))
            rest = rest[BLOCK:, BLOCK:] - dot(cross, cross, ((0,), (0,)))


def factorize(gram, own, step):
    root = float(RB * WIDTH * NX * NZ) ** 0.5
    f32 = jnp.float32
    vmem = pl.BlockSpec(memory_space=pltpu.VMEM)
    return pl.pallas_call(
        functools.partial(factor_kernel, step, root),
        out_shape=(
            jax.ShapeDtypeStruct((SHARE, WIDTH), f32),
            jax.ShapeDtypeStruct((WIDTH, WIDTH), f32),
        ),
        in_specs=[vmem, vmem],
        out_specs=(vmem, vmem),
        scratch_shapes=[pltpu.VMEM((BLOCK, 2 * BLOCK), f32), pltpu.VMEM((BLOCK, 2 * BLOCK), f32)],
        name="factorize",
    )(gram, own)


def local(sketch, blocks, block_rows, block_cols, counts):
    f32 = jnp.float32
    dma = pltpu.SemaphoreType.DMA
    vmem = pl.BlockSpec(memory_space=pltpu.VMEM)
    smem = pl.BlockSpec(memory_space=pltpu.SMEM)
    own, gram = pl.pallas_call(
        sketch_kernel,
        out_shape=(
            jax.ShapeDtypeStruct((SHARE, WIDTH), f32),
            jax.ShapeDtypeStruct((GROUP, 8, WIDTH), f32),
        ),
        in_specs=[smem, smem, smem, vmem, vmem],
        out_specs=(vmem, vmem),
        scratch_shapes=[
            pltpu.VMEM((NX, NZ, WIDTH, WIDTH), jnp.bfloat16),
            pltpu.VMEM((8, WIDTH, WIDTH), f32),
            pltpu.VMEM((RB, NC, SHARE, WIDTH), f32),
            pltpu.VMEM((RB, SHARE, WIDTH), f32),
            pltpu.VMEM((RB, SHARE, WIDTH), f32),
            pltpu.VMEM((NY - 1, SHARE, WIDTH), f32),
            pltpu.VMEM((GROUP, 8, WIDTH), f32),
            pltpu.VMEM((GROUP - 1, 8, WIDTH), f32),
            pltpu.VMEM((NZ, 8, WIDTH), f32),
            dma,
            dma((3,)), dma((3,)),
            dma((2, 8)), dma((2, 8)),
            dma((2, 8)), dma((2, 8)),
            dma((2, 2, 8)), dma((2, 2, 8)),
            dma((2, 8)), dma((2, 8)),
            dma((4,)), dma((4,)),
            dma((3,)), dma((3,)),
            dma((GROUP - 1,)), dma((GROUP - 1,)),
            dma((NZ,)), dma((NZ,)),
            dma((GROUP - 1,)), dma((GROUP - 1,)),
        ],
        compiler_params=pltpu.CompilerParams(collective_id=0, has_side_effects=True),
        name="sketch",
    )(block_rows, block_cols, counts, sketch, blocks)
    gram = gram.reshape(WIDTH, WIDTH)
    return factorize(gram, own, 8)


def solution(mesh):
    in_specs = (
        P(("rows", "cols"), None),
        P(("rows", "cols"), None, None),
        P(("rows", "cols")),
        P(("rows", "cols")),
        P(("rows", "cols")),
    )
    out_specs = (P(("rows", "cols"), None), P())
    return jax.shard_map(local, mesh=mesh, in_specs=in_specs, out_specs=out_specs, check_vma=False)
```

```python
import functools

import jax
import jax.numpy as jnp
from jax import lax
from jax.experimental import pallas as pl
from jax.experimental.pallas import tpu as pltpu
from jax.sharding import PartitionSpec as P

MESH = pl.DeviceIdType.MESH
HIGHEST = lax.Precision.HIGHEST
RB = 4
NX, NZ, NY, NC = 4, 16, 4, 2
WIDTH = 256
SPLIT = 80
GROUP = 32
SHARE = 128
BLOCK = 64


def copy_to(src, dst, send_sem, recv_sem, row, col):
    return pltpu.make_async_remote_copy(
        src_ref=src, dst_ref=dst, send_sem=send_sem, recv_sem=recv_sem,
        device_id=(row, col), device_id_type=MESH,
    )


def sketch_kernel(
    rows_ref, cols_ref, counts_ref, sketch_ref, blocks_ref, own_ref, gram_ref,
    panel, products, partial, received, half, received2, gram, slots, lows,
    local_sem, xa_send, xa_recv, za_send, za_recv, zb_send, zb_recv,
    xb_send, xb_recv, op_send, op_recv, c_send, c_recv, y_send, y_recv,
    g_send, g_recv, l_send, l_recv, s_send, s_recv,
):
    r = lax.axis_index("rows")
    c = lax.axis_index("cols")
    x, z = r // NZ, lax.rem(r, NZ)
    y, core = c // NC, lax.rem(c, NC)

    def at_x(k):
        return lax.rem(x + k, NX) * NZ + z

    def at_z(k):
        return x * NZ + lax.rem(z + k, NZ)

    cols = NY * NC
    me = x * cols + c

    def member(k):
        other = lax.rem(me + k, GROUP)
        return other, (other // cols) * NZ + z, lax.rem(other, cols)

    barrier = pltpu.get_barrier_semaphore()

    def hello(row, col):
        pl.semaphore_signal(barrier, inc=1, device_id=(row, col), device_id_type=MESH)

    for row in (at_z(1), at_z(NZ - 1), at_x(1), at_x(2), at_x(3)):
        hello(row, c)
    hello(r, y * NC + 1 - core)
    for k in (1, 2, 3):
        hello(r, lax.rem(y + k, NY) * NC + core)
    pl.semaphore_wait(barrier, 9)

    local = pltpu.make_async_copy(sketch_ref, panel.at[x, z], local_sem)
    local.start()

    first = pl.ds(0, SPLIT)
    second = pl.ds(SPLIT, WIDTH - SPLIT)

    def shifted(k):
        return lax.rem(z + k + NZ, NZ)

    def xa(k):
        piece = panel.at[x, z, first]
        return copy_to(sketch_ref.at[first], piece, xa_send.at[k - 1], xa_recv.at[k - 1], at_x(k), c)

    def za(side, hop):
        step = 1 - 2 * side
        piece = panel.at[:, shifted(-step * (hop - 1)), first]
        to = at_z(1 if side == 0 else NZ - 1)
        return copy_to(piece, piece, za_send.at[side, hop - 1], za_recv.at[side, hop - 1], to, c)

    def za_arrived(side, hop):
        step = 1 - 2 * side
        piece = panel.at[:, shifted(-step * hop), first]
        to = at_z(1 if side == 0 else NZ - 1)
        copy_to(piece, piece, za_send.at[side, hop - 1], za_recv.at[side, hop - 1], to, c).wait_recv()

    def zb(side, hop):
        step = 1 - 2 * side
        piece = panel.at[x, shifted(-step * (hop - 1)), second]
        to = at_z(1 if side == 0 else NZ - 1)
        return copy_to(piece, piece, zb_send.at[side, hop - 1], zb_recv.at[side, hop - 1], to, c)

    def zb_arrived(side, hop):
        step = 1 - 2 * side
        piece = panel.at[x, shifted(-step * hop), second]
        to = at_z(1 if side == 0 else NZ - 1)
        copy_to(piece, piece, zb_send.at[side, hop - 1], zb_recv.at[side, hop - 1], to, c).wait_recv()

    def piece_of(family, slot, column):
        at = shifted(-slot - 1) if family == 0 else shifted(slot)
        return panel.at[column, at, second]

    def xb(family, slot, way):
        piece = piece_of(family, slot, x)
        to = at_x(1 if way == 0 else NX - 1)
        return copy_to(piece, piece, xb_send.at[family, way, slot], xb_recv.at[family, way, slot], to, c)

    def xb_arrived(family, slot, way):
        column = lax.rem(x + (NX - 1 if way == 0 else 1), NX)
        piece = piece_of(family, slot, column)
        to = at_x(1 if way == 0 else NX - 1)
        copy_to(piece, piece, xb_send.at[family, way, slot], xb_recv.at[family, way, slot], to, c).wait_recv()

    def op(family, slot):
        column = lax.rem(x + (NX - 1 if family == 0 else 1), NX)
        piece = piece_of(family, slot, column)
        to = at_x(1 if family == 0 else NX - 1)
        return copy_to(piece, piece, op_send.at[family, slot], op_recv.at[family, slot], to, c)

    def op_arrived(family, slot):
        piece = piece_of(family, slot, lax.rem(x + 2, NX))
        to = at_x(1 if family == 0 else NX - 1)
        copy_to(piece, piece, op_send.at[family, slot], op_recv.at[family, slot], to, c).wait_recv()

    for k in (1, 2, 3):
        xa(k).start()
    local.wait()
    for side in (0, 1):
        zb(side, 1).start()
    for way in (0, 1):
        xb(1, 0, way).start()
    for k in (1, 2, 3):
        piece = panel.at[lax.rem(x + NX - k, NX), z, first]
        copy_to(piece, piece, xa_send.at[k - 1], xa_recv.at[k - 1], at_x(k), c).wait_recv()
    for side in (0, 1):
        za(side, 1).start()

    def hop_body(hop, carry):
        zb_arrived(0, hop)
        zb(0, hop + 1).start()
        for way in (0, 1):
            xb(0, hop - 1, way).start()
        zb_arrived(1, hop)

        @pl.when(hop < 7)
        def _():
            zb(1, hop + 1).start()

        for way in (0, 1):
            xb(1, hop, way).start()
        za_arrived(1, hop)
        za(1, hop + 1).start()
        za_arrived(0, hop)

        @pl.when(hop < 7)
        def _():
            za(0, hop + 1).start()

        xb_arrived(1, hop - 1, 1)
        op(1, hop - 1).start()

        @pl.when(hop > 1)
        def _():
            xb_arrived(0, hop - 2, 0)
            op(0, hop - 2).start()

        return carry

    lax.fori_loop(1, 8, hop_body, 0)
    zb_arrived(0, 8)
    for way in (0, 1):
        xb(0, 7, way).start()
    xb_arrived(1, 7, 1)
    op(1, 7).start()
    xb_arrived(0, 6, 0)
    op(0, 6).start()
    xb_arrived(0, 7, 0)
    op(0, 7).start()
    za_arrived(1, 8)

    def arrived(slot, carry):
        xb_arrived(0, slot, 1)
        xb_arrived(1, slot, 0)
        for family in (0, 1):
            op_arrived(family, slot)
        return carry

    lax.fori_loop(0, 8, arrived, 0)

    live = counts_ref[0]

    def slot_body(s, carry):
        q = cols_ref[s]
        products[s] = jnp.dot(
            blocks_ref[s], panel[q // NZ, lax.rem(q, NZ)], preferred_element_type=jnp.float32
        )
        return carry

    lax.fori_loop(0, 8, slot_body, 0)

    def pair(b):
        return copy_to(
            partial.at[b, 1 - core], received.at[b], c_send.at[b], c_recv.at[b], r, y * NC + 1 - core
        )

    def to_y(k):
        other = lax.rem(y + k, NY)
        return copy_to(
            half.at[other], received2.at[k - 1], y_send.at[k - 1], y_recv.at[k - 1], r, other * NC + core
        )

    def finish(k):
        b = lax.rem(y + k, NY)
        pair(b).wait_recv()
        half[b] = partial[b, core] + received[b]
        if k:
            to_y(k).start()

    order = (2, 1, 3, 0)
    for place, k in enumerate(order):
        b = lax.rem(y + k, NY)
        for part in range(NC):
            total = jnp.zeros((SHARE, WIDTH), jnp.float32)
            for s in range(8):
                weight = jnp.where(jnp.logical_and(rows_ref[s] == b, s < live), 1.0, 0.0)
                total = total + weight * products[s, part * SHARE:(part + 1) * SHARE]
            partial[b, part] = total
        pair(b).start()
        if place:
            finish(order[place - 1])
    finish(0)
    for k in (1, 2, 3):
        to_y(k).wait_recv()
    own = half[y] + received2[0] + received2[1] + received2[2]
    own_ref[...] = own
    gram[...] = lax.dot_general(
        own, own, (((0,), (0,)), ((), ())), precision=HIGHEST, preferred_element_type=jnp.float32
    ).reshape(GROUP, 8, WIDTH)

    def scatter(k):
        other, row, col = member(k)
        return copy_to(gram.at[other], slots.at[k - 1], g_send.at[k - 1], g_recv.at[k - 1], row, col)

    def line(i, source):
        hops = 8 - i // 2
        k = lax.rem(i, 2) * (NZ - 2 * hops) + hops
        return copy_to(lows.at[source(k)], lows.at[source(k)], l_send.at[i], l_recv.at[i], at_z(k), c)

    def spread(k, source):
        _, row, col = member(k)
        piece = gram_ref.at[source]
        return copy_to(piece, piece, s_send.at[k - 1], s_recv.at[k - 1], row, col)

    def each(stop, act):
        def body(k, carry):
            act(k)
            return carry
        lax.fori_loop(1, stop, body, 0)

    each(GROUP, lambda k: scatter(k).start())
    each(GROUP, lambda k: scatter(k).wait_recv())
    def along(act):
        def body(i, carry):
            act(i)
            return carry
        lax.fori_loop(1, NZ, body, 0)

    lows[z] = gram[me] + jnp.sum(slots[...], axis=0)
    along(lambda i: line(i, lambda k: z).start())
    along(lambda i: line(i, lambda k: lax.rem(z + NZ - k, NZ)).wait_recv())
    gram_ref[me] = jnp.sum(lows[...], axis=0)
    each(GROUP, lambda k: spread(k, me).start())

    def drain(slot, carry):
        for family in (0, 1):
            op(family, slot).wait_send()
            for way in (0, 1):
                xb(family, slot, way).wait_send()
        zb(0, slot + 1).wait_send()
        za(1, slot + 1).wait_send()

        @pl.when(slot < 7)
        def _():
            zb(1, slot + 1).wait_send()
            za(0, slot + 1).wait_send()

        return carry

    lax.fori_loop(0, 8, drain, 0)
    for k in (1, 2, 3):
        xa(k).wait_send()
    for k in range(NY):
        pair(k).wait_send()
    for k in (1, 2, 3):
        to_y(k).wait_send()
    each(GROUP, lambda k: scatter(k).wait_send())
    along(lambda i: line(i, lambda k: z).wait_send())
    each(GROUP, lambda k: spread(k, lax.rem(me + GROUP - k, GROUP)).wait_recv())
    each(GROUP, lambda k: spread(k, me).wait_send())


def factor_kernel(step, root, gram_ref, own_ref, basis_ref, factor_ref, work, rows):
    f32 = jnp.float32
    lane = lax.broadcasted_iota(jnp.int32, (1, 2 * BLOCK), 1)
    row_index = lax.broadcasted_iota(jnp.int32, (BLOCK, BLOCK), 0)
    lane_index = lax.broadcasted_iota(jnp.int32, (BLOCK, BLOCK), 1)
    below = row_index > lane_index
    eye = (row_index == lane_index).astype(f32)

    def dot(a, b, dims):
        return lax.dot_general(a, b, (dims, ((), ())), precision=HIGHEST, preferred_element_type=f32)

    def pick(value, j):
        return jnp.sum(jnp.where(lane == j, value, 0.0), axis=1, keepdims=True)

    def eliminate(block):
        work[...] = jnp.concatenate([block, eye], axis=1)

        def body(i, carry):
            j = i * step
            line = [work[pl.ds(j + t, 1), :] for t in range(step)]
            column = [pick(work[...], j + t) for t in range(step)]
            entry = [[pick(line[t], j + u) for u in range(step)] for t in range(step)]
            scaled = []
            for t in range(step):
                inverse = 1.0 / entry[t][t]
                for u in range(t + 1, step):
                    ratio = entry[t][u] * inverse
                    line[u] = line[u] - ratio * line[t]
                    column[u] = column[u] - ratio * column[t]
                    for v in range(u, step):
                        entry[u][v] = entry[u][v] - ratio * entry[t][v]
                scaled.append(line[t] * inverse)
            total = work[...]
            for t in range(step):
                total = total - column[t] * scaled[t]
            work[...] = total
            for t in range(step):
                rows[pl.ds(j + t, 1), :] = line[t] * (1.0 / jnp.sqrt(entry[t][t]))
            return carry

        lax.fori_loop(0, BLOCK // step, body, 0)
        return jnp.where(below, 0.0, rows[:, :BLOCK]), rows[:, BLOCK:]

    rest, share = gram_ref[...], own_ref[...]
    for first in range(0, WIDTH, BLOCK):
        last = first + BLOCK
        upper, inverse = eliminate(rest[:BLOCK, :BLOCK])
        factor_ref[first:last, first:last] = upper * (1.0 / root)
        if first:
            factor_ref[first:last, :first] = jnp.zeros((BLOCK, first), f32)
        solved = dot(share[:, :BLOCK], inverse, ((1,), (1,)))
        basis_ref[:, first:last] = solved * root
        if last < WIDTH:
            cross = dot(inverse, rest[:BLOCK, BLOCK:], ((1,), (0,)))
            factor_ref[first:last, last:] = cross * (1.0 / root)
            share = share[:, BLOCK:] - dot(solved, cross, ((1,), (0,)))
            rest = rest[BLOCK:, BLOCK:] - dot(cross, cross, ((0,), (0,)))


def factorize(gram, own, step):
    root = float(RB * WIDTH * NX * NZ) ** 0.5
    f32 = jnp.float32
    vmem = pl.BlockSpec(memory_space=pltpu.VMEM)
    return pl.pallas_call(
        functools.partial(factor_kernel, step, root),
        out_shape=(
            jax.ShapeDtypeStruct((SHARE, WIDTH), f32),
            jax.ShapeDtypeStruct((WIDTH, WIDTH), f32),
        ),
        in_specs=[vmem, vmem],
        out_specs=(vmem, vmem),
        scratch_shapes=[pltpu.VMEM((BLOCK, 2 * BLOCK), f32), pltpu.VMEM((BLOCK, 2 * BLOCK), f32)],
        name="factorize",
    )(gram, own)


def local(sketch, blocks, block_rows, block_cols, counts):
    f32 = jnp.float32
    dma = pltpu.SemaphoreType.DMA
    vmem = pl.BlockSpec(memory_space=pltpu.VMEM)
    smem = pl.BlockSpec(memory_space=pltpu.SMEM)
    own, gram = pl.pallas_call(
        sketch_kernel,
        out_shape=(
            jax.ShapeDtypeStruct((SHARE, WIDTH), f32),
            jax.ShapeDtypeStruct((GROUP, 8, WIDTH), f32),
        ),
        in_specs=[smem, smem, smem, vmem, vmem],
        out_specs=(vmem, vmem),
        scratch_shapes=[
            pltpu.VMEM((NX, NZ, WIDTH, WIDTH), jnp.bfloat16),
            pltpu.VMEM((8, WIDTH, WIDTH), f32),
            pltpu.VMEM((RB, NC, SHARE, WIDTH), f32),
            pltpu.VMEM((RB, SHARE, WIDTH), f32),
            pltpu.VMEM((RB, SHARE, WIDTH), f32),
            pltpu.VMEM((NY - 1, SHARE, WIDTH), f32),
            pltpu.VMEM((GROUP, 8, WIDTH), f32),
            pltpu.VMEM((GROUP - 1, 8, WIDTH), f32),
            pltpu.VMEM((NZ, 8, WIDTH), f32),
            dma,
            dma((3,)), dma((3,)),
            dma((2, 8)), dma((2, 8)),
            dma((2, 8)), dma((2, 8)),
            dma((2, 2, 8)), dma((2, 2, 8)),
            dma((2, 8)), dma((2, 8)),
            dma((4,)), dma((4,)),
            dma((3,)), dma((3,)),
            dma((GROUP - 1,)), dma((GROUP - 1,)),
            dma((NZ,)), dma((NZ,)),
            dma((GROUP - 1,)), dma((GROUP - 1,)),
        ],
        compiler_params=pltpu.CompilerParams(collective_id=0, has_side_effects=True),
        name="sketch",
    )(block_rows, block_cols, counts, sketch, blocks)
    gram = gram.reshape(WIDTH, WIDTH)
    return factorize(gram, own, 8)


def solution(mesh):
    in_specs = (
        P(("rows", "cols"), None),
        P(("rows", "cols"), None, None),
        P(("rows", "cols")),
        P(("rows", "cols")),
        P(("rows", "cols")),
    )
    out_specs = (P(("rows", "cols"), None), P())
    return jax.shard_map(local, mesh=mesh, in_specs=in_specs, out_specs=out_specs, check_vma=False)
```
